128 devices in a mesh: row: 8 (over x, core), col: 16 (over z, y).
Axes of the slice: x: 4, y: 4, z: 4, core: 2. Of those that a mesh axis runs over, the one named last changes fastest.
Arguments:
- luminance: float32 [1024, 8192], P('row', 'col'), may hold values from 0 to 1
- level_gain: float32 [5], replicated, may hold values from 0.5 to 2
Outputs:
- tone_mapped: float32 [1024, 8192], P('row', 'col')
The draws below stay inside these ranges and needn't reach their ends.
All inputs are finite; a program needn't handle non-finite values.
Results may differ from the reference program's by a relative error of at most 0.00002.
Values sent between devices are 32-bit elements; how exact they have to be, the bound alone decides.
No kernel may reach another device: no remote copies, remote signals or barrier semaphores. Data moves between devices by JAX's collectives and lax.ppermute only.
A program may use at most 64 MiB of HBM per device.

```python
import math
import jax
import jax.numpy as jnp
from jax import lax

CHANNELS = 16
LEVELS = 6
ROWS = 1024
COLS = 8192


def block_scale(own_key, extent, split, least, top_value):
    gain = 1.0
    for dim, blocks in split:
        steps = jax.random.uniform(jax.random.fold_in(jax.random.fold_in(own_key, 6), dim), (blocks,), jnp.float32, least / len(split), top_value / len(split))
        gain = gain * jnp.repeat(jnp.exp(steps), extent[dim] // blocks).reshape((-1,) + (1,) * (len(extent) - 1 - dim))
    return gain


def setup_inputs(seed: int = 0) -> dict:
    key_of = jax.random.split(jax.random.key(seed), 3)
    luminance = jnp.clip(1.0 * jax.random.uniform(key_of[0], (ROWS, COLS), jnp.float32) ** block_scale(key_of[0], (ROWS, COLS), ((0, 8), (1, 16)), -0.2, 0.2), 0.0, 1.0)
    level_gain = jnp.clip(jnp.exp(jax.random.uniform(key_of[1], (LEVELS - 1,), jnp.float32, math.log(0.5), math.log(2.0))), 0.5, 2.0)
    return dict(luminance=luminance, level_gain=level_gain)


binomial = (0.0625, 0.25, 0.375, 0.25, 0.0625)
detail_boost = 1.0
base_slope = 0.5
spread_inverse = 1.0 / (2.0 * 0.025 * 0.025)


def remap_tone(values, anchor, switch):
    offset = values - anchor
    return values + switch * ((base_slope - 1.0) * offset + detail_boost * offset * jnp.exp(-offset * offset * spread_inverse))


def hat_weights(guidance, anchor):
    return jnp.maximum(0.0, 1.0 - jnp.abs(guidance - anchor) * (CHANNELS - 1))


def down_valid(padded):
    out_rows = (padded.shape[-2] - 4) // 2
    blurred = binomial[0] * padded[..., 0:2 * out_rows - 1:2, :]
    for step in range(1, 5):
        blurred = blurred + binomial[step] * padded[..., step:step + 2 * out_rows - 1:2, :]
    out_cols = (padded.shape[-1] - 4) // 2
    result = binomial[0] * blurred[..., 0:2 * out_cols - 1:2]
    for step in range(1, 5):
        result = result + binomial[step] * blurred[..., step:step + 2 * out_cols - 1:2]
    return result


def up_valid(coarse):
    rows_in = coarse.shape[-2]
    even_rows = (coarse[..., 0:rows_in - 2, :] + 6.0 * coarse[..., 1:rows_in - 1, :] + coarse[..., 2:rows_in, :]) * 0.125
    odd_rows = (coarse[..., 1:rows_in - 1, :] + coarse[..., 2:rows_in, :]) * 0.5
    joined = jnp.stack([even_rows, odd_rows], axis=-2)
    joined = joined.reshape(joined.shape[:-3] + (2 * (rows_in - 2), joined.shape[-1]))
    cols_in = joined.shape[-1]
    even_cols = (joined[..., 0:cols_in - 2] + 6.0 * joined[..., 1:cols_in - 1] + joined[..., 2:cols_in]) * 0.125
    odd_cols = (joined[..., 1:cols_in - 1] + joined[..., 2:cols_in]) * 0.5
    result = jnp.stack([even_cols, odd_cols], axis=-1)
    return result.reshape(result.shape[:-2] + (2 * (cols_in - 2),))


def down_wrap(values):
    return down_valid(jnp.pad(values, ((2, 2), (2, 2)), mode="wrap"))


def up_wrap(values):
    return up_valid(jnp.pad(values, ((1, 1), (1, 1)), mode="wrap"))


def reference(luminance, level_gain):
    guides = [luminance]
    for level_index in range(LEVELS - 1):
        guides.append(down_wrap(guides[-1]))

    def channel_step(totals, channel_index):
        anchor = channel_index.astype(jnp.float32) / (CHANNELS - 1)
        current = remap_tone(luminance, anchor, 1.0)
        new_totals = []
        for level_index in range(LEVELS - 1):
            coarse = down_wrap(current)
            detail = current - up_wrap(coarse)
            new_totals.append(totals[level_index] + hat_weights(guides[level_index], anchor) * detail)
            current = coarse
        return tuple(new_totals), None

    initial = tuple(jnp.zeros_like(guides[level_index]) for level_index in range(LEVELS - 1))
    totals, unused = lax.scan(channel_step, initial, jnp.arange(CHANNELS, dtype=jnp.int32))
    result = guides[LEVELS - 1]
    for level_index in reversed(range(LEVELS - 1)):
        result = level_gain[level_index] * totals[level_index] + up_wrap(result)
    return result
```

```python
import math

import jax
import jax.numpy as jnp
from jax import lax
from jax.experimental import pallas as pl
from jax.experimental.pallas import tpu as pltpu
from jax.sharding import PartitionSpec as P


ROWS = 320
LANES = 128
HALF = 8
STEP = 1.0 / 15.0
BETA = math.sqrt(800.0 * math.log2(math.e))
F32 = jnp.float32


def iota(shape, dim):
    return lax.broadcasted_iota(jnp.int32, shape, dim)


def left(x, n=1):
    return pltpu.roll(x, LANES - n, axis=x.ndim - 1)


def right(x, n=1):
    return pltpu.roll(x, n, axis=x.ndim - 1)


def pick(x, idx):
    return jnp.take_along_axis(x, idx, axis=1)


def select_columns(x, table):
    hi = x.astype(jnp.bfloat16)
    rest = x - hi.astype(F32)
    mid = rest.astype(jnp.bfloat16)
    low = (rest - mid.astype(F32)).astype(jnp.bfloat16)
    dot = lambda part: jnp.dot(part, table, preferred_element_type=F32)
    return dot(hi) + dot(mid) + dot(low)


def spread(ref, *index):
    return ref[index[:-1] + (pl.ds(index[-1], HALF, stride=0), slice(None))]


def fold(y0, y1, y2, y3, y4):
    return (y0 + y4) + 6.0 * y2 + 4.0 * (y1 + y3)


def bump(lum, anchor):
    u = lum - anchor
    return u * jnp.exp2(-(u * u))


def columns_from_four(y):
    y0, y1, y2, y3 = y
    return (
        fold(right(y2), right(y3), y0, y1, y2),
        fold(y0, y1, y2, y3, left(y0)),
    )


def columns_from_two(y):
    y0, y1 = y
    return fold(right(y0), right(y1), y0, y1, left(y0))


def columns_strided(y, n):
    return fold(right(y, 2 * n), right(y, n), y, left(y, n), left(y, 2 * n))


def channel_chain(lum, anchors, d1, d2, d3):
    groups = len(anchors)

    def row(e):
        values = [spread(lum, c, e) for c in range(4)]
        return [[bump(v, a) for v in values] for a in anchors]

    def step(i, state):
        pair, even, odd_before = state
        odd = row(2 * i + 1)
        even_next = row(2 * i + 2)
        new_pair = [[None] * 4 for g in range(groups)]
        for g in range(groups):
            y = []
            for c in range(4):
                new_pair[g][c] = even[g][c] + even_next[g][c]
                y.append(
                    (pair[g][c] + new_pair[g][c])
                    + 4.0 * (even[g][c] + (odd_before[g][c] + odd[g][c]))
                )
            out = columns_from_four(y)
            d1[i, 2 * g] = out[0]
            d1[i, 2 * g + 1] = out[1]
        return new_pair, even_next, odd

    def body(t, state):
        state = step(2 * t + 1, state)
        return step(2 * t + 2, state)

    first = row(0)
    second = row(2)
    pair = [[a + b for a, b in zip(x, y)] for x, y in zip(first, second)]
    lax.fori_loop(0, 79, body, (pair, second, row(1)))

    def second_level(i, carry):
        for g in range(groups):
            y = [fold(*[d1[2 * i + s - 2, 2 * g + c] for s in range(5)]) for c in range(2)]
            d2[i, g] = columns_from_two(y)
        return carry

    lax.fori_loop(2, 79, second_level, 0)

    def third_level(i, carry):
        for g in range(groups):
            d3[i, g] = columns_strided(fold(*[d2[2 * i + s - 2, g] for s in range(5)]), 1)
        return carry

    lax.fori_loop(2, 39, third_level, 0)


def rows_blurred(ref, c, base, count):
    return fold(*[ref[c, pl.ds(base + s - 2, count, stride=2), :] for s in range(5)])


def guide_chain(lum, scale, g1, g2, g3):
    def first(t, carry):
        i = 8 * t + 8
        y = [rows_blurred(lum, c, 2 * i, 8) for c in range(4)]
        out = columns_from_four(y)
        g1[0, pl.ds(i, 8), :] = out[0] * (scale / 256.0)
        g1[1, pl.ds(i, 8), :] = out[1] * (scale / 256.0)
        return carry

    lax.fori_loop(0, 18, first, 0)
    for i in (1, 151):
        y = [rows_blurred(lum, c, 2 * i, 8) for c in range(4)]
        out = columns_from_four(y)
        g1[0, i : i + 8, :] = out[0] * (scale / 256.0)
        g1[1, i : i + 8, :] = out[1] * (scale / 256.0)
    for i in (2, 8, 16, 24, 32, 40, 48, 56, 64, 71):
        y = [rows_blurred(g1, c, 2 * i, 8) for c in range(2)]
        g2[0, i : i + 8, :] = columns_from_two(y) * (1.0 / 256.0)
    for i in (2, 8, 16, 24, 31):
        g3[i : i + 8, :] = columns_strided(rows_blurred(g2, 0, 2 * i, 8), 1) * (1.0 / 256.0)


def anchor_tile(base):
    return (iota((HALF, LANES), 0) + base).astype(F32)


def kernel_a(top, mid, bottom, d1, d2, d3, x15, g1, g2, g3, base_term, lum):
    source = iota((512, 512), 0)
    target = iota((512, 512), 1)
    table = jnp.where(source == 4 * (target % LANES) + target // LANES, 1.0, 0.0).astype(jnp.bfloat16)
    for ref, start, count in ((top, 0, 96), (mid, 96, 128), (bottom, 224, 96)):
        phases = select_columns(ref[...], table)
        for c in range(4):
            part = phases[:, c * LANES : (c + 1) * LANES]
            lum[c, start : start + count, :] = part * BETA
            if start == 96:
                x15[c] = part * 15.0
    guide_chain(lum, 1.0 / BETA, g1, g2, g3)
    anchors = [anchor_tile(HALF * g) * (BETA * STEP) for g in range(2)]
    channel_chain(lum, anchors, d1, d2, d3)

    def natural(t, carry):
        rows = pl.ds(pl.multiple_of(8 * t, 8), 8)
        value = mid[rows, :]
        place = value * 15.0
        lower = jnp.floor(place)
        part = place - lower
        near = value - lower * STEP
        far = value - (lower + 1.0) * STEP
        bend = (1.0 - part) * near * jnp.exp(near * near * -800.0) + part * far * jnp.exp(far * far * -800.0)
        base_term[rows, :] = 0.5 * value + bend
        return carry

    lax.fori_loop(0, 16, natural, 0)


def hat(place, channel):
    return jnp.maximum(0.0, 1.0 - jnp.abs(place - channel))


def total(x):
    return jnp.sum(x, axis=0, keepdims=True)


def rows_up(before, here, after):
    later = here + after
    return here + 0.25 * ((before + here) + later), later


def tiles(ref, index, count):
    return [ref[index + (slice(8 * t, 8 * t + 8), slice(None))] for t in range(count)]


def kernel_b(
    gain_ref, far_left, near_left, near_right, far_right, d1, d2, d3, x15, g1, g2, g3, base_term, out,
    lum, s1, s2, s3, h1, h2, h3, f1, f2, b3, b4, b5, e3, e4, e5,
    c4, c3, c2a, c2s, c1a, c1s, r5, r4, u4, r3, u3, w2, r2a, r2s, wide_a, wide_s, k1, k2, rest,
):
    gains = [gain_ref[i] for i in range(5)]
    lane = iota((HALF, LANES), 1)
    channel = [anchor_tile(HALF * g) for g in range(2)]
    split = anchor_tile(0) + jnp.where(lane >= 64, 8.0, 0.0)

    source = iota((512, 512), 0)
    target = iota((512, 512), 1)
    wanted = 32 + 320 * ((target // 32) % 2) + 4 * (target % 32) + target // LANES
    table = jnp.where(source == wanted, 1.0, 0.0).astype(jnp.bfloat16)
    for start in range(0, ROWS, 160):
        part = slice(start, start + 160)
        natural = jnp.concatenate(
            [far_left[part, :], near_left[part, :], near_right[part, :], far_right[part, :]], axis=1
        )
        phases = select_columns(natural, table)
        for c in range(4):
            lum[c, part, :] = phases[:, c * LANES : (c + 1) * LANES] * BETA
    guide_chain(lum, 1.0 / BETA, h1, h2, h3)
    channel_chain(lum, [split * (BETA * STEP)], s1, s2, s3)

    first, last = lane == 0, lane == 127
    ends = first | last
    low_ends = ends | (lane == 1)
    at = lambda base, table, other: base + sum(
        (jnp.where(lane == k, v - other, 0) for k, v in table.items()), jnp.zeros_like(lane) + other
    )
    one_same = [at(64 * g, {0: 24, 127: 40}, 24) for g in range(2)]
    one_other = [at(64 * g, {0: 23, 127: 39}, 23) for g in range(2)]
    two_same = [at(64 * g, {0: 24, 1: 25, 127: 39}, 24) for g in range(2)]
    two_other = [at(64 * g, {0: 23, 127: 40}, 23) for g in range(2)]

    def edges_one(q0, q1, t0, t1, g):
        a, b = pick(t0, one_same[g]), pick(t1, one_other[g])
        q0 = jnp.where(first, a, q0)
        q1 = jnp.where(last, b, q1)
        return jnp.where(first, b, right(q1)), q0, q1, jnp.where(last, a, left(q0))

    def edges_two(y, t, g):
        a, b = pick(t, two_same[g]), pick(t, two_other[g])
        y = jnp.where(low_ends, a, y)
        return jnp.where(first, b, right(y)), y, jnp.where(last, b, left(y))

    def fix_one(i, carry):
        for g in range(2):
            found = edges_one(d1[i, 2 * g], d1[i, 2 * g + 1], s1[i, 0], s1[i, 1], g)
            for n in range(4):
                f1[i, 4 * g + n] = found[n]
        return carry

    lax.fori_loop(46, 114, fix_one, 0)

    def fix_two(i, carry):
        for g in range(2):
            found = edges_two(d2[i, g], s2[i, 0], g)
            for n in range(3):
                f2[i, 3 * g + n] = found[n]
        return carry

    lax.fori_loop(22, 59, fix_two, 0)

    for t in range(5, 15):
        rows = slice(8 * t, 8 * t + 8)
        m, q0, q1, p = edges_one(g1[0, rows, :], g1[1, rows, :], h1[0, rows, :], h1[1, rows, :], 0)
        k1[0, rows, :], k1[1, rows, :] = q0, q1
    for t in range(2, 8):
        rows = slice(8 * t, 8 * t + 8)
        k2[rows, :] = edges_two(g2[0, rows, :], h2[0, rows, :], 0)[1]

    from_a = (lane >= 14) & (lane <= 74)
    index_a = jnp.clip(2 * (lane - 12), 0, 127)
    index_s = [jnp.clip(64 * g + jnp.where(lane < 14, 2 * lane, 2 * lane - 112), 0, 127) for g in range(2)]

    def merge(i, carry):
        for g in range(2):
            b3[i, g] = jnp.where(from_a, pick(d3[i, g], index_a), pick(s3[i, 0], index_s[g])) * (
                1.0 / (BETA * 2.0**24)
            )
        return carry

    lax.fori_loop(2, 39, merge, 0)
    for t in range(5):
        rows = slice(8 * t, 8 * t + 8)
        e3[rows, :] = jnp.where(from_a, pick(g3[rows, :], index_a), pick(h3[rows, :], index_s[0]))

    def fourth_level(i, carry):
        for g in range(2):
            b4[i, g] = columns_strided(fold(*[b3[2 * i + s - 2, g] for s in range(5)]), 1) * (1.0 / 256.0)
        return carry

    lax.fori_loop(2, 19, fourth_level, 0)

    def fifth_level(i, carry):
        for g in range(2):
            b5[i, g] = columns_strided(fold(*[b4[2 * i + s - 2, g] for s in range(5)]), 2) * (1.0 / 256.0)
        return carry

    lax.fori_loop(2, 9, fifth_level, 0)
    blur = lambda ref, i: fold(*[ref[pl.ds(2 * i + s - 2, 8, stride=2), :] for s in range(5)])
    for i in (2, 8, 11):
        e4[i : i + 8, :] = columns_strided(blur(e3, i), 1) * (1.0 / 256.0)
    e5[2:10, :] = columns_strided(blur(e4, 2), 2) * (1.0 / 256.0)

    def lanes_up(y, n):
        even = 0.125 * (right(y, n) + left(y, n)) + 0.75 * y
        odd = 0.5 * (right(y, n // 2) + left(y, n // 2))
        return even, odd

    def on_grid(y, n, parity):
        even, odd = lanes_up(y, n)
        return jnp.where(parity, odd, even)

    parity_four = (lane % 4) != 0
    parity_three = (lane % 2) != 0

    def coefficient_b(fine, coarse, guide, sums, n, parity):
        def body(i, carry):
            made = []
            for g in range(2):
                made.append(rows_up(coarse[i - 1, g], coarse[i, g], coarse[i + 1, g]))
            for odd in range(2):
                x = 2 * i + odd
                place = spread(guide, x) * 15.0
                acc = None
                for g in range(2):
                    part = hat(place, channel[g]) * (fine[x, g] - 0.5 * on_grid(made[g][odd], n, parity))
                    acc = part if acc is None else acc + part
                sums[pl.ds(x, 1), :] = total(acc)
            return carry

        return body

    lax.fori_loop(2, 8, coefficient_b(b4, b5, e4, c4, 4, parity_four), 0)
    lax.fori_loop(5, 15, coefficient_b(b3, b4, e3, c3, 2, parity_three), 0)

    def raise_rows(src, dst, start, count, index=()):
        above = src[index + (pl.ds(start - 1, count), slice(None))]
        here = src[index + (pl.ds(start, count), slice(None))]
        below = src[index + (pl.ds(start + 1, count), slice(None))]
        even, odd = rows_up(above, here, below)
        dst[index + (pl.ds(2 * start, count, stride=2), slice(None))] = 0.5 * even
        dst[index + (pl.ds(2 * start + 1, count, stride=2), slice(None))] = 0.5 * odd

    r5[...] = e5[...] * (1.0 - 0.5 * gains[4])
    raise_rows(r5, u4, 1, 8)
    for t in range(3):
        rows = slice(8 * t, 8 * t + 8)
        value = gains[4] * (0.5 * e4[rows, :] + c4[rows, :]) + on_grid(u4[rows, :], 4, parity_four)
        r4[rows, :] = value - (0.5 * gains[3]) * e4[rows, :]
    raise_rows(r4, u3, 4, 8)
    raise_rows(r4, u3, 8, 8)
    for t in range(1, 4):
        rows = slice(8 * t, 8 * t + 8)
        value = gains[3] * (0.5 * e3[rows, :] + c3[rows, :]) + on_grid(u3[rows, :], 2, parity_three)
        r3[rows, :] = value - (0.5 * gains[2]) * e3[rows, :]

    base_a = lane // 2 + 12
    column_s = jnp.where((lane // 32) % 2 == 0, lane % 32 - 24 + 256, lane % 32 + 120 + 256)
    base_s = column_s // 2 - 128 + 12
    odd_column = (lane % 2) != 0
    clip = lambda x: jnp.clip(x, 0, 127)
    three_a = [clip(base_a + d) for d in (-1, 0, 1)]
    three_s = [clip(base_s + d) for d in (-1, 0, 1)]
    upper_half = lane >= 64

    def expand(y, three):
        m, c, p = [pick(y, t) for t in three]
        return jnp.where(odd_column, 0.5 * (c + p), 0.125 * (m + p) + 0.75 * c)

    scale_two = 1.0 / (BETA * 2.0**16)

    def coefficient_two(i, carry):
        made = [rows_up(b3[i - 1, g], b3[i, g], b3[i + 1, g]) for g in range(2)]
        for odd in range(2):
            x = 2 * i + odd
            place = spread(k2, x) * 15.0
            acc = None
            for g in range(2):
                part = hat(place, channel[g]) * (
                    f2[x, 3 * g + 1] * scale_two - 0.5 * expand(made[g][odd], three_a)
                )
                acc = part if acc is None else acc + part
            c2a[pl.ds(x, 1), :] = total(acc)
            place = spread(h2, 0, x) * 15.0
            wide = jnp.where(upper_half, expand(made[1][odd], three_s), expand(made[0][odd], three_s))
            acc = hat(place, split) * (s2[x, 0] * scale_two - 0.5 * wide)
            acc = acc + right(acc, 64)
            c2s[pl.ds(x, 1), :] = total(acc)
        return carry

    lax.fori_loop(11, 29, coefficient_two, 0)
    for start in (8, 16, 24):
        raise_rows(r3, w2, start, 8)
    for t in range(2, 8):
        rows = slice(8 * t, 8 * t + 8)
        coarse = w2[rows, :]
        value = gains[2] * (0.5 * k2[rows, :] + c2a[rows, :]) + expand(coarse, three_a)
        r2a[rows, :] = value - (0.5 * gains[1]) * k2[rows, :]
        guide = h2[0, rows, :]
        value = gains[2] * (0.5 * guide + c2s[rows, :]) + expand(coarse, three_s)
        r2s[rows, :] = value - (0.5 * gains[1]) * guide

    def two_phases(m, y, p):
        return y + 0.25 * ((m + y) + (y + p)), y + p

    def coefficient_one(i, carry):
        made = [[rows_up(f2[i - 1, n], f2[i, n], f2[i + 1, n]) for n in range(3 * g, 3 * g + 3)] for g in range(2)]
        made_s = rows_up(s2[i - 1, 0], s2[i, 0], s2[i + 1, 0])
        for odd in range(2):
            x = 2 * i + odd
            places = [spread(k1, c, x) * 15.0 for c in range(2)]
            acc = [None, None]
            for g in range(2):
                ups = two_phases(*[made[g][n][odd] for n in range(3)])
                for c in range(2):
                    part = hat(places[c], channel[g]) * (f1[x, 4 * g + 1 + c] * 1024.0 - ups[c])
                    acc[c] = part if acc[c] is None else acc[c] + part
            for c in range(2):
                c1a[c, pl.ds(x, 1), :] = total(acc[c])
            ups = two_phases(right(made_s[odd]), made_s[odd], left(made_s[odd]))
            for c in range(2):
                part = hat(spread(h1, c, x) * 15.0, split) * (s1[x, c] * 1024.0 - ups[c])
                c1s[c, pl.ds(x, 1), :] = total(part + right(part, 64))
        return carry

    lax.fori_loop(23, 57, coefficient_one, 0)
    scale_one = gains[1] * (1.0 / (BETA * 2.0**18))
    for start in (20, 28, 36, 44, 52):
        raise_rows(r2a, wide_a, start, 8)
        raise_rows(r2s, wide_s, start, 8)

    def collapse_one(t, carry):
        rows = pl.ds(pl.multiple_of(8 * t, 8), 8)
        y, z = wide_a[rows, :], wide_s[rows, :]
        m, y, p = edges_two(y, z, 0)
        ups_a = two_phases(m, y, p)
        ups_s = two_phases(right(z), z, left(z))
        found = []
        for c in range(2):
            guide = k1[c, rows, :]
            found.append(
                (0.5 * (gains[1] - gains[0])) * guide + scale_one * c1a[c, rows, :] + 0.5 * ups_a[c]
            )
        side = []
        for c in range(2):
            guide = h1[c, rows, :]
            side.append((0.5 * (gains[1] - gains[0])) * guide + scale_one * c1s[c, rows, :] + 0.5 * ups_s[c])
        found = edges_one(found[0], found[1], side[0], side[1], 0)
        for n in range(4):
            rest_in[n, rows, :] = found[n]
        return carry

    rest_in = lum
    lax.fori_loop(5, 15, collapse_one, 0)

    scale_zero = gains[0] * (1.0 / (BETA * 2.0**10))

    def four_phases(m, q0, q1, p):
        t0, t1, tm = q0 + q1, q1 + p, m + q0
        return q0 + 0.25 * (tm + t0), t0, q1 + 0.25 * (t0 + t1), t1

    def coefficient_zero(i, carry):
        made = [[rows_up(f1[i - 1, n], f1[i, n], f1[i + 1, n]) for n in range(4 * g, 4 * g + 4)] for g in range(2)]
        for odd in range(2):
            x = 2 * (i - 48) + odd
            ups = [four_phases(*[made[g][n][odd] for n in range(4)]) for g in range(2)]
            for c in range(4):
                place = spread(x15, c, x)
                acc = hat(place, channel[0]) * ups[0][c] + hat(place, channel[1]) * ups[1][c]
                rest[c, pl.ds(x, 1), :] = total(acc)
        return carry

    lax.fori_loop(48, 112, coefficient_zero, 0)

    inverse = jnp.where(target == 4 * (source % LANES) + source // LANES, 1.0, 0.0).astype(jnp.bfloat16)
    for start in range(0, 64, 32):
        above = [rest_in[n, 47 + start : 79 + start, :] for n in range(4)]
        here = [rest_in[n, 48 + start : 80 + start, :] for n in range(4)]
        below = [rest_in[n, 49 + start : 81 + start, :] for n in range(4)]
        made = [rows_up(a, b, c) for a, b, c in zip(above, here, below)]
        for odd in range(2):
            ups = four_phases(*[m[odd] for m in made])
            for c in range(4):
                at_rows = pl.ds(2 * start + odd, 32, stride=2)
                rest[c, at_rows, :] = 0.25 * ups[c] - scale_zero * rest[c, at_rows, :]
    phases = jnp.concatenate([rest[c] for c in range(4)], axis=1)
    out[...] = select_columns(phases, inverse) + gains[0] * base_term[...]


def shape(*dims):
    return jax.ShapeDtypeStruct(dims, F32)


def vmem(*dims):
    return pltpu.VMEM(dims, F32)


def run_a(top, mid, bottom):
    whole = pl.BlockSpec(memory_space=pltpu.VMEM)
    return pl.pallas_call(
        kernel_a,
        out_shape=(
            shape(160, 4, HALF, LANES),
            shape(80, 2, HALF, LANES),
            shape(40, 2, HALF, LANES),
            shape(4, 128, LANES),
            shape(2, 160, LANES),
            shape(1, 80, LANES),
            shape(40, LANES),
            shape(128, 512),
        ),
        in_specs=[whole] * 3,
        out_specs=(whole,) * 8,
        scratch_shapes=[vmem(4, ROWS, LANES)],
        compiler_params=pltpu.CompilerParams(vmem_limit_bytes=40 << 20),
        cost_estimate=pl.CostEstimate(flops=60_000_000, transcendentals=2_600_000, bytes_accessed=6_000_000),
    )(top, mid, bottom)


def run_b(gain, strips, parts):
    whole = pl.BlockSpec(memory_space=pltpu.VMEM)
    return pl.pallas_call(
        kernel_b,
        out_shape=shape(128, 512),
        in_specs=[pl.BlockSpec(memory_space=pltpu.SMEM)] + [whole] * 12,
        out_specs=whole,
        scratch_shapes=[
            vmem(4, ROWS, LANES),
            vmem(160, 2, HALF, LANES),
            vmem(80, 1, HALF, LANES),
            vmem(40, 1, HALF, LANES),
            vmem(2, 160, LANES),
            vmem(1, 80, LANES),
            vmem(40, LANES),
            vmem(160, 8, HALF, LANES),
            vmem(80, 6, HALF, LANES),
            vmem(40, 2, HALF, LANES),
            vmem(24, 2, HALF, LANES),
            vmem(16, 2, HALF, LANES),
            vmem(40, LANES),
            vmem(24, LANES),
            vmem(16, LANES),
            vmem(24, LANES),
            vmem(40, LANES),
            vmem(80, LANES),
            vmem(80, LANES),
            vmem(2, 160, LANES),
            vmem(2, 160, LANES),
            vmem(16, LANES),
            vmem(24, LANES),
            vmem(24, LANES),
            vmem(40, LANES),
            vmem(40, LANES),
            vmem(80, LANES),
            vmem(80, LANES),
            vmem(80, LANES),
            vmem(160, LANES),
            vmem(160, LANES),
            vmem(2, 160, LANES),
            vmem(80, LANES),
            vmem(4, 128, LANES),
        ],
        compiler_params=pltpu.CompilerParams(vmem_limit_bytes=48 << 20),
        cost_estimate=pl.CostEstimate(flops=60_000_000, transcendentals=1_300_000, bytes_accessed=6_000_000),
    )(gain, *strips, *parts)


def ring(axis, shift):
    count = lax.axis_size(axis)
    return [(i, (i + shift) % count) for i in range(count)]


def local(luminance, level_gain):
    top = lax.ppermute(luminance[32:], "row", ring("row", 1))
    bottom = lax.ppermute(luminance[:96], "row", ring("row", -1))
    near = []
    for columns in (slice(0, LANES), slice(512 - LANES, 512)):
        near.append(jnp.concatenate([x[:, columns] for x in (top, luminance, bottom)], axis=0))
    far_left = lax.ppermute(near[1], "col", ring("col", 1))
    far_right = lax.ppermute(near[0], "col", ring("col", -1))
    parts = run_a(top, luminance, bottom)
    return run_b(level_gain, (far_left, near[0], near[1], far_right), parts)


def solution(mesh):
    return jax.shard_map(
        local, mesh=mesh, in_specs=(P("row", "col"), P()), out_specs=P("row", "col"), check_vma=False
    )
```

```python
import math

import jax
import jax.numpy as jnp
from jax import lax
from jax.experimental import pallas as pl
from jax.experimental.pallas import tpu as pltpu
from jax.sharding import PartitionSpec as P


ROWS = 320
LANES = 128
HALF = 8
STEP = 1.0 / 15.0
BETA = math.sqrt(800.0 * math.log2(math.e))
F32 = jnp.float32


def iota(shape, dim):
    return lax.broadcasted_iota(jnp.int32, shape, dim)


def left(x, n=1):
    return pltpu.roll(x, LANES - n, axis=x.ndim - 1)


def right(x, n=1):
    return pltpu.roll(x, n, axis=x.ndim - 1)


def pick(x, idx):
    return jnp.take_along_axis(x, idx, axis=1)


def select_columns(x, table):
    hi = x.astype(jnp.bfloat16)
    rest = x - hi.astype(F32)
    mid = rest.astype(jnp.bfloat16)
    low = (rest - mid.astype(F32)).astype(jnp.bfloat16)
    dot = lambda part: jnp.dot(part, table, preferred_element_type=F32)
    return dot(hi) + dot(mid) + dot(low)


def spread(ref, *index):
    return ref[index[:-1] + (pl.ds(index[-1], HALF, stride=0), slice(None))]


def fold(y0, y1, y2, y3, y4):
    return (y0 + y4) + 6.0 * y2 + 4.0 * (y1 + y3)


def bump(lum, anchor):
    u = lum - anchor
    return u * jnp.exp2(-(u * u))


def columns_from_four(y):
    y0, y1, y2, y3 = y
    return (
        fold(right(y2), right(y3), y0, y1, y2),
        fold(y0, y1, y2, y3, left(y0)),
    )


def columns_from_two(y):
    y0, y1 = y
    return fold(right(y0), right(y1), y0, y1, left(y0))


def columns_strided(y, n):
    return fold(right(y, 2 * n), right(y, n), y, left(y, n), left(y, 2 * n))


def loop(low, high, size, body, state=()):
    whole = (high - low) // size

    def several(t, state):
        for n in range(size):
            state = body(low + size * t + n, state)
        return state

    state = lax.fori_loop(0, whole, several, state)
    for i in range(low + size * whole, high):
        state = body(i, state)
    return state


def channel_chain(lum, anchors, d1, d2, d3):
    groups = len(anchors)

    def row(e):
        values = [spread(lum, c, e) for c in range(4)]
        return [[bump(v, a) for v in values] for a in anchors]

    def step(i, state):
        pair, even, odd_before = state
        odd = row(2 * i + 1)
        even_next = row(2 * i + 2)
        new_pair = [[None] * 4 for g in range(groups)]
        for g in range(groups):
            y = []
            for c in range(4):
                new_pair[g][c] = even[g][c] + even_next[g][c]
                y.append(
                    (pair[g][c] + new_pair[g][c])
                    + 4.0 * (even[g][c] + (odd_before[g][c] + odd[g][c]))
                )
            out = columns_from_four(y)
            d1[i, 2 * g] = out[0]
            d1[i, 2 * g + 1] = out[1]
        return new_pair, even_next, odd

    first = row(2)
    second = row(4)
    pair = [[a + b for a, b in zip(x, y)] for x, y in zip(first, second)]
    loop(2, 159, 16 // groups, step, (pair, second, row(3)))

    def second_level(i, carry):
        for g in range(groups):
            y = [fold(*[d1[2 * i + s - 2, 2 * g + c] for s in range(5)]) for c in range(2)]
            d2[i, g] = columns_from_two(y)
        return carry

    loop(2, 79, 16 // groups, second_level)

    def third_level(i, carry):
        for g in range(groups):
            d3[i, g] = columns_strided(fold(*[d2[2 * i + s - 2, g] for s in range(5)]), 1)
        return carry

    loop(2, 39, 16 // groups, third_level)


def rows_blurred(ref, c, base, count):
    return fold(*[ref[c, pl.ds(base + s - 2, count, stride=2), :] for s in range(5)])


def guide_chain(lum, scale, g1, g2, g3):
    def first(t, carry):
        i = pl.multiple_of(8 * t, 8) + 8
        y = [rows_blurred(lum, c, 2 * i, 8) for c in range(4)]
        out = columns_from_four(y)
        g1[0, pl.ds(i, 8), :] = out[0] * (scale / 256.0)
        g1[1, pl.ds(i, 8), :] = out[1] * (scale / 256.0)
        return carry

    loop(0, 18, 6, first)
    for i in (1, 151):
        y = [rows_blurred(lum, c, 2 * i, 8) for c in range(4)]
        out = columns_from_four(y)
        g1[0, i : i + 8, :] = out[0] * (scale / 256.0)
        g1[1, i : i + 8, :] = out[1] * (scale / 256.0)
    for i in (2, 8, 16, 24, 32, 40, 48, 56, 64, 71):
        y = [rows_blurred(g1, c, 2 * i, 8) for c in range(2)]
        g2[0, i : i + 8, :] = columns_from_two(y) * (1.0 / 256.0)
    for i in (2, 8, 16, 24, 31):
        g3[i : i + 8, :] = columns_strided(rows_blurred(g2, 0, 2 * i, 8), 1) * (1.0 / 256.0)


def anchor_tile(base):
    return (iota((HALF, LANES), 0) + base).astype(F32)


def kernel_a(top, mid, bottom, d1, d2, d3, x15, g1, g2, g3, base_term, lum):
    source = iota((512, 512), 0)
    target = iota((512, 512), 1)
    table = jnp.where(source == 4 * (target % LANES) + target // LANES, 1.0, 0.0).astype(jnp.bfloat16)
    for ref, start, count in ((top, 0, 96), (mid, 96, 128), (bottom, 224, 96)):
        phases = select_columns(ref[...], table)
        for c in range(4):
            part = phases[:, c * LANES : (c + 1) * LANES]
            lum[c, start : start + count, :] = part * BETA
            if start == 96:
                x15[c] = part * 15.0
    guide_chain(lum, 1.0 / BETA, g1, g2, g3)
    anchors = [anchor_tile(HALF * g) * (BETA * STEP) for g in range(2)]
    channel_chain(lum, anchors, d1, d2, d3)

    def natural(t, carry):
        rows = pl.ds(pl.multiple_of(8 * t, 8), 8)
        value = mid[rows, :]
        place = value * 15.0
        lower = jnp.floor(place)
        part = place - lower
        near = value - lower * STEP
        far = value - (lower + 1.0) * STEP
        bend = (1.0 - part) * near * jnp.exp(near * near * -800.0) + part * far * jnp.exp(far * far * -800.0)
        base_term[rows, :] = 0.5 * value + bend
        return carry

    loop(0, 16, 4, natural)


def hat(place, channel):
    return jnp.maximum(0.0, 1.0 - jnp.abs(place - channel))


def eight_totals(parts):
    sublane = iota((HALF, LANES), 0)

    def join(a, b, offset, span):
        mine = (sublane - offset + HALF) % (2 * span) < span
        return jnp.where(mine, a, b) + pltpu.roll(jnp.where(mine, b, a), HALF - span, axis=0)

    def four(a, b, c, d, offset):
        return join(join(a, b, offset, 4), join(c, d, offset + 2, 4), offset, 2)

    x = parts
    return join(four(x[0], x[4], x[2], x[6], 0), four(x[1], x[5], x[3], x[7], 1), 0, 1)


def rows_up(before, here, after):
    later = here + after
    return here + 0.25 * ((before + here) + later), later


def tiles(ref, index, count):
    return [ref[index + (slice(8 * t, 8 * t + 8), slice(None))] for t in range(count)]


def kernel_b(
    gain_ref, far_left, near_left, near_right, far_right, d1, d2, d3, x15, g1, g2, g3, base_term, out,
    lum, s1, s2, s3, h1, h2, h3, f1, f2, b3, b4, b5, e3, e4, e5,
    c4, c3, c2a, c2s, c1a, c1s, r5, r4, u4, r3, u3, wide3, w2, r2a, r2s, wide_a, wide_s, k1, k2, rest,
):
    gains = [gain_ref[i] for i in range(5)]
    lane = iota((HALF, LANES), 1)
    channel = [anchor_tile(HALF * g) for g in range(2)]
    split = anchor_tile(0) + jnp.where(lane >= 64, 8.0, 0.0)

    source = iota((512, 512), 0)
    target = iota((512, 512), 1)
    wanted = 32 + 320 * ((target // 32) % 2) + 4 * (target % 32) + target // LANES
    table = jnp.where(source == wanted, 1.0, 0.0).astype(jnp.bfloat16)
    for start in range(0, ROWS, 160):
        part = slice(start, start + 160)
        natural = jnp.concatenate(
            [far_left[part, :], near_left[part, :], near_right[part, :], far_right[part, :]], axis=1
        )
        phases = select_columns(natural, table)
        for c in range(4):
            lum[c, part, :] = phases[:, c * LANES : (c + 1) * LANES] * BETA
    guide_chain(lum, 1.0 / BETA, h1, h2, h3)
    channel_chain(lum, [split * (BETA * STEP)], s1, s2, s3)

    first, last, low_ends = lane == 0, lane == 127, lane <= 1
    turn = lambda x, source, to: pltpu.roll(x, (to - source) % LANES, axis=1)

    def edges_one(q0, q1, t0, t1, g):
        base = 64 * g
        q0 = jnp.where(first, turn(t0, base + 24, 0), q0)
        q1 = jnp.where(last, turn(t1, base + 39, 127), q1)
        before = jnp.where(first, turn(t1, base + 23, 0), right(q1))
        after = jnp.where(last, turn(t0, base + 40, 127), left(q0))
        return before, q0, q1, after

    def edges_two(y, t, g):
        base = 64 * g
        y = jnp.where(last, turn(t, base + 39, 127), jnp.where(low_ends, turn(t, base + 24, 0), y))
        before = jnp.where(first, turn(t, base + 23, 0), right(y))
        after = jnp.where(last, turn(t, base + 40, 127), left(y))
        return before, y, after

    def fix_one(i, carry):
        for g in range(2):
            found = edges_one(d1[i, 2 * g], d1[i, 2 * g + 1], s1[i, 0], s1[i, 1], g)
            for n in range(4):
                f1[i, 4 * g + n] = found[n]
        return carry

    loop(46, 114, 4, fix_one)

    def fix_two(i, carry):
        for g in range(2):
            found = edges_two(d2[i, g], s2[i, 0], g)
            for n in range(3):
                f2[i, 3 * g + n] = found[n]
        return carry

    loop(22, 59, 4, fix_two)

    for t in range(5, 15):
        rows = slice(8 * t, 8 * t + 8)
        m, q0, q1, p = edges_one(g1[0, rows, :], g1[1, rows, :], h1[0, rows, :], h1[1, rows, :], 0)
        k1[0, rows, :], k1[1, rows, :] = q0, q1
    for t in range(2, 8):
        rows = slice(8 * t, 8 * t + 8)
        k2[rows, :] = edges_two(g2[0, rows, :], h2[0, rows, :], 0)[1]

    from_a = (lane >= 14) & (lane <= 74)
    index_a = jnp.clip(2 * (lane - 12), 0, 127)
    index_s = [jnp.clip(64 * g + jnp.where(lane < 14, 2 * lane, 2 * lane - 112), 0, 127) for g in range(2)]

    def merge(i, carry):
        for g in range(2):
            b3[i, g] = jnp.where(from_a, pick(d3[i, g], index_a), pick(s3[i, 0], index_s[g])) * (
                1.0 / (BETA * 2.0**24)
            )
        return carry

    loop(2, 39, 8, merge)
    for t in range(5):
        rows = slice(8 * t, 8 * t + 8)
        e3[rows, :] = jnp.where(from_a, pick(g3[rows, :], index_a), pick(h3[rows, :], index_s[0]))

    def fourth_level(i, carry):
        for g in range(2):
            b4[i, g] = columns_strided(fold(*[b3[2 * i + s - 2, g] for s in range(5)]), 1) * (1.0 / 256.0)
        return carry

    loop(2, 19, 17, fourth_level)

    def fifth_level(i, carry):
        for g in range(2):
            b5[i, g] = columns_strided(fold(*[b4[2 * i + s - 2, g] for s in range(5)]), 2) * (1.0 / 256.0)
        return carry

    loop(2, 9, 7, fifth_level)
    blur = lambda ref, i: fold(*[ref[pl.ds(2 * i + s - 2, 8, stride=2), :] for s in range(5)])
    for i in (2, 8, 11):
        e4[i : i + 8, :] = columns_strided(blur(e3, i), 1) * (1.0 / 256.0)
    e5[2:10, :] = columns_strided(blur(e4, 2), 2) * (1.0 / 256.0)

    def lanes_up(y, n):
        even = 0.125 * (right(y, n) + left(y, n)) + 0.75 * y
        odd = 0.5 * (right(y, n // 2) + left(y, n // 2))
        return even, odd

    def on_grid(y, n, parity):
        even, odd = lanes_up(y, n)
        return jnp.where(parity, odd, even)

    parity_four = (lane % 4) != 0
    parity_three = (lane % 2) != 0

    def coefficient_b(fine, coarse, guide, sums, start, n, parity):
        parts = []
        for i in range(start // 2, start // 2 + 4):
            made = [rows_up(coarse[i - 1, g], coarse[i, g], coarse[i + 1, g]) for g in range(2)]
            for odd in range(2):
                x = 2 * i + odd
                place = spread(guide, x) * 15.0
                terms = [
                    hat(place, channel[g]) * (fine[x, g] - 0.5 * on_grid(made[g][odd], n, parity)) for g in range(2)
                ]
                parts.append(terms[0] + terms[1])
        sums[start : start + 8, :] = eight_totals(parts)

    for start in (4, 12):
        coefficient_b(b4, b5, e4, c4, start, 4, parity_four)
    for start in (10, 18, 26):
        coefficient_b(b3, b4, e3, c3, start, 2, parity_three)

    def raise_rows(src, dst, start, count, index=()):
        above = src[index + (pl.ds(start - 1, count), slice(None))]
        here = src[index + (pl.ds(start, count), slice(None))]
        below = src[index + (pl.ds(start + 1, count), slice(None))]
        even, odd = rows_up(above, here, below)
        dst[index + (pl.ds(2 * start, count, stride=2), slice(None))] = 0.5 * even
        dst[index + (pl.ds(2 * start + 1, count, stride=2), slice(None))] = 0.5 * odd

    r5[...] = e5[...] * (1.0 - 0.5 * gains[4])
    raise_rows(r5, u4, 1, 8)
    for t in range(3):
        rows = slice(8 * t, 8 * t + 8)
        value = gains[4] * (0.5 * e4[rows, :] + c4[rows, :]) + on_grid(u4[rows, :], 4, parity_four)
        r4[rows, :] = value - (0.5 * gains[3]) * e4[rows, :]
    raise_rows(r4, u3, 4, 8)
    raise_rows(r4, u3, 8, 8)
    for t in range(1, 4):
        rows = slice(8 * t, 8 * t + 8)
        value = gains[3] * (0.5 * e3[rows, :] + c3[rows, :]) + on_grid(u3[rows, :], 2, parity_three)
        r3[rows, :] = value - (0.5 * gains[2]) * e3[rows, :]

    base_a = lane // 2 + 12
    column_s = jnp.where((lane // 32) % 2 == 0, lane % 32 - 24 + 256, lane % 32 + 120 + 256)
    base_s = column_s // 2 - 128 + 12
    odd_column = (lane % 2) != 0
    clip = lambda x: jnp.clip(x, 0, 127)
    base_a, base_s = clip(base_a), clip(base_s)
    upper_half = lane >= 64

    def expand(y, at):
        even, odd = 0.125 * (right(y) + left(y)) + 0.75 * y, 0.5 * (y + left(y))
        return jnp.where(odd_column, pick(odd, at), pick(even, at))

    scale_two = 2.0 / (BETA * 2.0**16)

    def widen(i, carry):
        for g in range(2):
            wide3[i, g] = expand(b3[i, g], base_a)
        wide3[i, 2] = jnp.where(upper_half, expand(b3[i, 1], base_s), expand(b3[i, 0], base_s))
        return carry

    loop(10, 32, 11, widen)

    def coefficient_two(t, carry):
        parts, side = [], []
        for n in range(4):
            i = 4 * t + 11 + n
            made = [rows_up(wide3[i - 1, g], wide3[i, g], wide3[i + 1, g]) for g in range(3)]
            for odd in range(2):
                x = 2 * i + odd
                place = spread(k2, x) * 15.0
                terms = [
                    hat(place, channel[g]) * (f2[x, 3 * g + 1] * scale_two - made[g][odd]) for g in range(2)
                ]
                parts.append(terms[0] + terms[1])
                place = spread(h2, 0, x) * 15.0
                side.append(hat(place, split) * (s2[x, 0] * scale_two - made[2][odd]))
        rows = pl.ds(8 * t + 22, 8)
        c2a[rows, :] = 0.5 * eight_totals(parts)
        both = eight_totals(side)
        c2s[rows, :] = 0.5 * (both + right(both, 64))
        return carry

    lax.fori_loop(0, 5, coefficient_two, 0)
    for start in (8, 16, 24):
        raise_rows(r3, w2, start, 8)
    for t in range(2, 8):
        rows = slice(8 * t, 8 * t + 8)
        coarse = w2[rows, :]
        value = gains[2] * (0.5 * k2[rows, :] + c2a[rows, :]) + expand(coarse, base_a)
        r2a[rows, :] = value - (0.5 * gains[1]) * k2[rows, :]
        guide = h2[0, rows, :]
        value = gains[2] * (0.5 * guide + c2s[rows, :]) + expand(coarse, base_s)
        r2s[rows, :] = value - (0.5 * gains[1]) * guide

    def two_phases(m, y, p):
        return y + 0.25 * ((m + y) + (y + p)), y + p

    def coefficient_one(t, carry):
        parts, side = [[], []], [[], []]
        for n in range(4):
            i = 4 * t + 23 + n
            made = [
                [rows_up(f2[i - 1, m], f2[i, m], f2[i + 1, m]) for m in range(3 * g, 3 * g + 3)] for g in range(2)
            ]
            made_s = rows_up(s2[i - 1, 0], s2[i, 0], s2[i + 1, 0])
            for odd in range(2):
                x = 2 * i + odd
                ups = [two_phases(*[made[g][m][odd] for m in range(3)]) for g in range(2)]
                ups_s = two_phases(right(made_s[odd]), made_s[odd], left(made_s[odd]))
                for c in range(2):
                    place = spread(k1, c, x) * 15.0
                    terms = [hat(place, channel[g]) * (f1[x, 4 * g + 1 + c] * 1024.0 - ups[g][c]) for g in range(2)]
                    parts[c].append(terms[0] + terms[1])
                    place = spread(h1, c, x) * 15.0
                    side[c].append(hat(place, split) * (s1[x, c] * 1024.0 - ups_s[c]))
        rows = pl.ds(8 * t + 46, 8)
        for c in range(2):
            c1a[c, rows, :] = eight_totals(parts[c])
            both = eight_totals(side[c])
            c1s[c, rows, :] = both + right(both, 64)
        return carry

    lax.fori_loop(0, 9, coefficient_one, 0)
    scale_one = gains[1] * (1.0 / (BETA * 2.0**18))
    for start in (20, 28, 36, 44, 52):
        raise_rows(r2a, wide_a, start, 8)
        raise_rows(r2s, wide_s, start, 8)

    def collapse_one(t, carry):
        rows = pl.ds(pl.multiple_of(8 * t, 8), 8)
        y, z = wide_a[rows, :], wide_s[rows, :]
        m, y, p = edges_two(y, z, 0)
        ups_a = two_phases(m, y, p)
        ups_s = two_phases(right(z), z, left(z))
        found = []
        for c in range(2):
            guide = k1[c, rows, :]
            found.append(
                (0.5 * (gains[1] - gains[0])) * guide + scale_one * c1a[c, rows, :] + 0.5 * ups_a[c]
            )
        side = []
        for c in range(2):
            guide = h1[c, rows, :]
            side.append((0.5 * (gains[1] - gains[0])) * guide + scale_one * c1s[c, rows, :] + 0.5 * ups_s[c])
        found = edges_one(found[0], found[1], side[0], side[1], 0)
        for n in range(4):
            rest_in[n, rows, :] = found[n]
        return carry

    rest_in = lum
    loop(5, 15, 5, collapse_one)

    scale_zero = gains[0] * (1.0 / (BETA * 2.0**10))

    def four_phases(m, q0, q1, p):
        t0, t1, tm = q0 + q1, q1 + p, m + q0
        return q0 + 0.25 * (tm + t0), t0, q1 + 0.25 * (t0 + t1), t1

    def coefficient_zero(t, carry):
        parts = [[] for c in range(4)]
        for n in range(4):
            i = 4 * t + 48 + n
            made = [
                [rows_up(f1[i - 1, m], f1[i, m], f1[i + 1, m]) for m in range(4 * g, 4 * g + 4)] for g in range(2)
            ]
            for odd in range(2):
                ups = [four_phases(*[made[g][m][odd] for m in range(4)]) for g in range(2)]
                for c in range(4):
                    place = spread(x15, c, 8 * t + 2 * n + odd)
                    parts[c].append(hat(place, channel[0]) * ups[0][c] + hat(place, channel[1]) * ups[1][c])
        for c in range(4):
            rest[c, pl.ds(pl.multiple_of(8 * t, 8), 8), :] = eight_totals(parts[c])
        return carry

    lax.fori_loop(0, 16, coefficient_zero, 0)

    inverse = jnp.where(target == 4 * (source % LANES) + source // LANES, 1.0, 0.0).astype(jnp.bfloat16)
    for start in range(0, 64, 32):
        above = [rest_in[n, 47 + start : 79 + start, :] for n in range(4)]
        here = [rest_in[n, 48 + start : 80 + start, :] for n in range(4)]
        below = [rest_in[n, 49 + start : 81 + start, :] for n in range(4)]
        made = [rows_up(a, b, c) for a, b, c in zip(above, here, below)]
        for odd in range(2):
            ups = four_phases(*[m[odd] for m in made])
            for c in range(4):
                at_rows = pl.ds(2 * start + odd, 32, stride=2)
                rest[c, at_rows, :] = 0.25 * ups[c] - scale_zero * rest[c, at_rows, :]
    phases = jnp.concatenate([rest[c] for c in range(4)], axis=1)
    out[...] = select_columns(phases, inverse) + gains[0] * base_term[...]


def shape(*dims):
    return jax.ShapeDtypeStruct(dims, F32)


def vmem(*dims):
    return pltpu.VMEM(dims, F32)


def run_a(top, mid, bottom):
    whole = pl.BlockSpec(memory_space=pltpu.VMEM)
    return pl.pallas_call(
        kernel_a,
        out_shape=(
            shape(160, 4, HALF, LANES),
            shape(80, 2, HALF, LANES),
            shape(40, 2, HALF, LANES),
            shape(4, 128, LANES),
            shape(2, 160, LANES),
            shape(1, 80, LANES),
            shape(40, LANES),
            shape(128, 512),
        ),
        in_specs=[whole] * 3,
        out_specs=(whole,) * 8,
        scratch_shapes=[vmem(4, ROWS, LANES)],
        compiler_params=pltpu.CompilerParams(vmem_limit_bytes=40 << 20),
        cost_estimate=pl.CostEstimate(flops=60_000_000, transcendentals=2_600_000, bytes_accessed=6_000_000),
    )(top, mid, bottom)


def run_b(gain, strips, parts):
    whole = pl.BlockSpec(memory_space=pltpu.VMEM)
    return pl.pallas_call(
        kernel_b,
        out_shape=shape(128, 512),
        in_specs=[pl.BlockSpec(memory_space=pltpu.SMEM)] + [whole] * 12,
        out_specs=whole,
        scratch_shapes=[
            vmem(4, ROWS, LANES),
            vmem(160, 2, HALF, LANES),
            vmem(80, 1, HALF, LANES),
            vmem(40, 1, HALF, LANES),
            vmem(2, 160, LANES),
            vmem(1, 80, LANES),
            vmem(40, LANES),
            vmem(160, 8, HALF, LANES),
            vmem(80, 6, HALF, LANES),
            vmem(40, 2, HALF, LANES),
            vmem(24, 2, HALF, LANES),
            vmem(16, 2, HALF, LANES),
            vmem(40, LANES),
            vmem(24, LANES),
            vmem(16, LANES),
            vmem(24, LANES),
            vmem(40, LANES),
            vmem(80, LANES),
            vmem(80, LANES),
            vmem(2, 160, LANES),
            vmem(2, 160, LANES),
            vmem(16, LANES),
            vmem(24, LANES),
            vmem(24, LANES),
            vmem(40, LANES),
            vmem(40, LANES),
            vmem(40, 3, HALF, LANES),
            vmem(80, LANES),
            vmem(80, LANES),
            vmem(80, LANES),
            vmem(160, LANES),
            vmem(160, LANES),
            vmem(2, 160, LANES),
            vmem(80, LANES),
            vmem(4, 128, LANES),
        ],
        compiler_params=pltpu.CompilerParams(vmem_limit_bytes=48 << 20),
        cost_estimate=pl.CostEstimate(flops=60_000_000, transcendentals=1_300_000, bytes_accessed=6_000_000),
    )(gain, *strips, *parts)


def ring(axis, shift):
    count = lax.axis_size(axis)
    return [(i, (i + shift) % count) for i in range(count)]


def local(luminance, level_gain):
    top = lax.ppermute(luminance[32:], "row", ring("row", 1))
    bottom = lax.ppermute(luminance[:96], "row", ring("row", -1))
    near = []
    for columns in (slice(0, LANES), slice(512 - LANES, 512)):
        near.append(jnp.concatenate([x[:, columns] for x in (top, luminance, bottom)], axis=0))
    far_left = lax.ppermute(near[1], "col", ring("col", 1))
    far_right = lax.ppermute(near[0], "col", ring("col", -1))
    parts = run_a(top, luminance, bottom)
    return run_b(level_gain, (far_left, near[0], near[1], far_right), parts)


def solution(mesh):
    return jax.shard_map(
        local, mesh=mesh, in_specs=(P("row", "col"), P()), out_specs=P("row", "col"), check_vma=False
    )
```

```python
import math

import jax
import jax.numpy as jnp
from jax import lax
from jax.experimental import pallas as pl
from jax.experimental.pallas import tpu as pltpu
from jax.sharding import PartitionSpec as P


ROWS = 320
LANES = 128
HALF = 8
STEP = 1.0 / 15.0
BETA = math.sqrt(800.0 * math.log2(math.e))
F32 = jnp.float32
UNROLL = {1: 53, 2: 26}
UNROLL_TWO = {1: 39, 2: 26}
UNROLL_SUMS = 4


def iota(shape, dim):
    return lax.broadcasted_iota(jnp.int32, shape, dim)


def left(x, n=1):
    return pltpu.roll(x, LANES - n, axis=x.ndim - 1)


def right(x, n=1):
    return pltpu.roll(x, n, axis=x.ndim - 1)


def pick(x, idx):
    return jnp.take_along_axis(x, idx, axis=1)


def select_columns(x, table):
    hi = x.astype(jnp.bfloat16)
    rest = x - hi.astype(F32)
    mid = rest.astype(jnp.bfloat16)
    low = (rest - mid.astype(F32)).astype(jnp.bfloat16)
    count = x.shape[0]
    out = jnp.dot(jnp.concatenate([hi, mid, low], axis=0), table, preferred_element_type=F32)
    return out[:count] + out[count : 2 * count] + out[2 * count :]


def spread(ref, *index):
    return ref[index[:-1] + (pl.ds(index[-1], HALF, stride=0), slice(None))]


def fold(y0, y1, y2, y3, y4):
    return (y0 + y4) + 6.0 * y2 + 4.0 * (y1 + y3)


def bump(lum, anchor, power):
    u = lum - anchor
    return u * jnp.exp2(power - u * u)


def columns_from_four(y):
    y0, y1, y2, y3 = y
    return (
        (right(y2) + y2) + 6.0 * y0 + (right(y3) + y1),
        (y0 + left(y0)) + 6.0 * y2 + (y1 + y3),
    )


def columns_from_two(y):
    y0, y1 = y
    return fold(right(y0), right(y1), y0, y1, left(y0))


def columns_strided(y, n):
    return fold(right(y, 2 * n), right(y, n), y, left(y, n), left(y, 2 * n))


def loop(low, high, size, body, state=()):
    whole = (high - low) // size

    def several(t, state):
        for n in range(size):
            state = body(low + size * t + n, state)
        return state

    state = lax.fori_loop(0, whole, several, state)
    for i in range(low + size * whole, high):
        state = body(i, state)
    return state


def channel_chain(lum, anchors, d1, d2, d3):
    groups = len(anchors)

    def row(e, odd):
        values = [spread(lum, c, e) for c in range(4)]
        return [[bump(v, a, 2.0 * odd + 2.0 * (c % 2)) for c, v in enumerate(values)] for a in anchors]

    def step(i, state):
        even_before, even, odd_before = state
        odd = row(2 * i + 1, 1)
        even_next = row(2 * i + 2, 0)
        for g in range(groups):
            y = [
                (even_before[g][c] + even_next[g][c]) + 6.0 * even[g][c] + (odd_before[g][c] + odd[g][c])
                for c in range(4)
            ]
            out = columns_from_four(y)
            d1[i, 2 * g] = out[0]
            d1[i, 2 * g + 1] = out[1]
        return even, even_next, odd

    loop(2, 159, UNROLL[groups], step, (row(2, 0), row(4, 0), row(3, 1)))

    def second_level(i, carry):
        for g in range(groups):
            y = [fold(*[d1[2 * i + s - 2, 2 * g + c] for s in range(5)]) for c in range(2)]
            d2[i, g] = columns_from_two(y)
        return carry

    loop(2, 79, UNROLL_TWO[groups], second_level)

    def third_level(i, carry):
        for g in range(groups):
            d3[i, g] = columns_strided(fold(*[d2[2 * i + s - 2, g] for s in range(5)]), 1)
        return carry

    loop(2, 39, UNROLL_TWO[groups], third_level)


def rows_blurred(ref, c, base, count):
    return fold(*[ref[c, pl.ds(base + s - 2, count, stride=2), :] for s in range(5)])


def guide_chain(lum, scale, g1, g2, g3):
    def first(t, carry):
        i = pl.multiple_of(8 * t, 8) + 8
        y = [rows_blurred(lum, c, 2 * i, 8) * (1.0 + 3.0 * (c % 2)) for c in range(4)]
        out = columns_from_four(y)
        g1[0, pl.ds(i, 8), :] = out[0] * (scale / 256.0)
        g1[1, pl.ds(i, 8), :] = out[1] * (scale / 256.0)
        return carry

    loop(0, 18, 6, first)
    for i in (1, 151):
        y = [rows_blurred(lum, c, 2 * i, 8) * (1.0 + 3.0 * (c % 2)) for c in range(4)]
        out = columns_from_four(y)
        g1[0, i : i + 8, :] = out[0] * (scale / 256.0)
        g1[1, i : i + 8, :] = out[1] * (scale / 256.0)
    for i in (2, 8, 16, 24, 32, 40, 48, 56, 64, 71):
        y = [rows_blurred(g1, c, 2 * i, 8) for c in range(2)]
        g2[0, i : i + 8, :] = columns_from_two(y) * (1.0 / 256.0)
    for i in (2, 8, 16, 24, 31):
        g3[i : i + 8, :] = columns_strided(rows_blurred(g2, 0, 2 * i, 8), 1) * (1.0 / 256.0)


def anchor_tile(base):
    return (iota((HALF, LANES), 0) + base).astype(F32)


def kernel_a(top, mid, bottom, d1, d2, d3, x15, g1, g2, g3, base_term, lum):
    source = iota((256, 256), 0)
    target = iota((256, 256), 1)
    table = jnp.where(source == 4 * (target % 64) + target // 64, 1.0, 0.0).astype(jnp.bfloat16)
    for ref, skip, start, count in ((top, 32, 0, 96), (mid, 0, 96, 128), (bottom, 0, 224, 96)):
        both = jnp.concatenate([ref[skip : skip + count, :256], ref[skip : skip + count, 256:]], axis=0)
        split = select_columns(both, table)
        low_half = iota((count, LANES), 1) < 64
        for pair in range(2):
            a = split[:count, pair * LANES : (pair + 1) * LANES]
            b = split[count:, pair * LANES : (pair + 1) * LANES]
            for c, part in (
                (2 * pair, jnp.where(low_half, a, right(b, 64))),
                (2 * pair + 1, jnp.where(low_half, right(a, 64), b)),
            ):
                lum[c, start : start + count, :] = part * BETA
                if start == 96:
                    x15[c] = part * 15.0
    guide_chain(lum, 1.0 / BETA, g1, g2, g3)
    anchors = [anchor_tile(HALF * g) * (BETA * STEP) for g in range(2)]
    channel_chain(lum, anchors, d1, d2, d3)

    def natural(t, carry):
        rows = pl.ds(pl.multiple_of(8 * t, 8), 8)
        value = mid[rows, :]
        place = value * 15.0
        lower = jnp.floor(place)
        part = place - lower
        near = value - lower * STEP
        far = value - (lower + 1.0) * STEP
        bend = (1.0 - part) * near * jnp.exp(near * near * -800.0) + part * far * jnp.exp(far * far * -800.0)
        base_term[rows, :] = 0.5 * value + bend
        return carry

    loop(0, 16, 4, natural)


def hat(place, channel):
    return jnp.maximum(0.0, 1.0 - jnp.abs(place - channel))


def eight_totals(parts):
    sublane = iota((HALF, LANES), 0)

    def join(a, b, offset, span):
        mine = (sublane - offset + HALF) % (2 * span) < span
        return jnp.where(mine, a, b) + pltpu.roll(jnp.where(mine, b, a), HALF - span, axis=0)

    def four(a, b, c, d, offset):
        return join(join(a, b, offset, 4), join(c, d, offset + 2, 4), offset, 2)

    x = parts
    return join(four(x[0], x[4], x[2], x[6], 0), four(x[1], x[5], x[3], x[7], 1), 0, 1)


def rows_up(before, here, after):
    later = here + after
    return here + 0.25 * ((before + here) + later), later


def raised(rows):
    sums = [a + b for a, b in zip(rows, rows[1:])]
    out = []
    for n in range(1, len(rows) - 1):
        out += [rows[n] + 0.25 * (sums[n - 1] + sums[n]), sums[n]]
    return out


def two_phases(m, y, p):
    return y + 0.25 * ((m + y) + (y + p)), y + p


def four_phases(m, q0, q1, p):
    t0, t1, tm = q0 + q1, q1 + p, m + q0
    return q0 + 0.25 * (tm + t0), t0, q1 + 0.25 * (t0 + t1), t1


def kernel_c(d1, d2, x15, g1, sums, c1a):
    channel = [anchor_tile(HALF * g) for g in range(2)]

    def level_one(t, carry):
        parts = [[None] * 8 for c in range(2)]
        for g in range(2):
            rows = [d2[4 * t + 22 + n, g] for n in range(6)]
            fine = [raised(y) for y in ([right(y) for y in rows], rows, [left(y) for y in rows])]
            for n in range(8):
                ups = two_phases(*[f[n] for f in fine])
                for c in range(2):
                    x = 8 * t + 46 + n
                    part = hat(spread(g1, c, x) * 15.0, channel[g]) * (d1[x, 2 * g + c] * 1024.0 - ups[c])
                    parts[c][n] = part if g == 0 else parts[c][n] + part
        for c in range(2):
            c1a[c, pl.ds(8 * t + 46, 8), :] = eight_totals(parts[c])
        return carry

    loop(0, 9, UNROLL_SUMS, level_one)

    def level_zero(t, carry):
        parts = [[None] * 8 for c in range(4)]
        for g in range(2):
            rows = [[d1[4 * t + 47 + n, 2 * g + c] for n in range(6)] for c in range(2)]
            fine = [raised(y) for y in ([right(y) for y in rows[1]], rows[0], rows[1], [left(y) for y in rows[0]])]
            for n in range(8):
                ups = four_phases(*[f[n] for f in fine])
                for c in range(4):
                    part = hat(spread(x15, c, 8 * t + n), channel[g]) * ups[c]
                    parts[c][n] = part if g == 0 else parts[c][n] + part
        for c in range(4):
            sums[c, pl.ds(pl.multiple_of(8 * t, 8), 8), :] = eight_totals(parts[c])
        return carry

    loop(0, 16, UNROLL_SUMS, level_zero)


def kernel_b(
    gain_ref, top, mid, bottom, far_left, far_right, far_top, far_bottom,
    d2, d3, g1, g2, g3, base_term, sums, c1a, out,
    lum, s1, s2, s3, h1, h2, h3, b3, b4, b5, e3, e4, e5,
    c4, c3, c2a, c2s, c1s, sums_s, r5, r4, u4, r3, u3, wide3, w2, r2a, r2s, wide_a, wide_s, rest,
):
    gains = [gain_ref[i] for i in range(5)]
    lane = iota((HALF, LANES), 1)
    channel = [anchor_tile(HALF * g) for g in range(2)]
    split = anchor_tile(0) + jnp.where(lane >= 64, 8.0, 0.0)

    source = iota((512, 256), 0)
    target = iota((512, 256), 1)
    wanted = 32 + 320 * ((target // 32) % 2) + 4 * (target % 32) + target // 64
    table = jnp.where(source == wanted, 1.0, 0.0).astype(jnp.bfloat16)
    for natural, start, count in (
        ([far_top[:, :LANES], top[32:, :LANES], top[32:, 384:], far_top[:, LANES:]], 0, 96),
        ([far_left[...], mid[:, :LANES], mid[:, 384:], far_right[...]], 96, 128),
        ([far_bottom[:, :LANES], bottom[:96, :LANES], bottom[:96, 384:], far_bottom[:, LANES:]], 224, 96),
    ):
        pieces = select_columns(jnp.concatenate(natural, axis=1), table)
        low_half = iota((count, LANES), 1) < 64
        for pair in range(2):
            a = pieces[:, pair * LANES : (pair + 1) * LANES] * BETA
            b = right(a, 64)
            lum[2 * pair, start : start + count, :] = jnp.where(low_half, a, b)
            lum[2 * pair + 1, start : start + count, :] = jnp.where(low_half, b, a)
    guide_chain(lum, 1.0 / BETA, h1, h2, h3)
    channel_chain(lum, [split * (BETA * STEP)], s1, s2, s3)

    first, last = lane == 0, lane == 127
    turn = lambda x, source, to: pltpu.roll(x, (to - source) % LANES, axis=1)

    def ends(x, t, low, high):
        return jnp.where(lane >= high, turn(t, 39, 127), jnp.where(lane <= low, turn(t, 24, 0), x))

    def edges_one(q0, q1, t0, t1):
        q0, q1 = ends(q0, t0, 2, 126), ends(q1, t1, 2, 126)
        return jnp.where(first, turn(t1, 23, 0), right(q1)), q0, q1, jnp.where(last, turn(t0, 40, 127), left(q0))

    def edges_two(y, t):
        y = ends(y, t, 1, 127)
        return jnp.where(first, turn(t, 23, 0), right(y)), y, jnp.where(last, turn(t, 40, 127), left(y))

    from_a = (lane >= 14) & (lane <= 74)
    index_a = jnp.clip(2 * (lane - 12), 0, 127)
    index_s = [jnp.clip(64 * g + jnp.where(lane < 14, 2 * lane, 2 * lane - 112), 0, 127) for g in range(2)]

    def merge(i, carry):
        for g in range(2):
            b3[i, g] = jnp.where(from_a, pick(d3[i, g], index_a), pick(s3[i, 0], index_s[g])) * (
                1.0 / (BETA * 2.0**24)
            )
        return carry

    loop(2, 39, 8, merge)
    for t in range(5):
        rows = slice(8 * t, 8 * t + 8)
        e3[rows, :] = jnp.where(from_a, pick(g3[rows, :], index_a), pick(h3[rows, :], index_s[0]))

    def fourth_level(i, carry):
        for g in range(2):
            b4[i, g] = columns_strided(fold(*[b3[2 * i + s - 2, g] for s in range(5)]), 1) * (1.0 / 256.0)
        return carry

    loop(2, 19, 17, fourth_level)

    def fifth_level(i, carry):
        for g in range(2):
            b5[i, g] = columns_strided(fold(*[b4[2 * i + s - 2, g] for s in range(5)]), 2) * (1.0 / 256.0)
        return carry

    loop(2, 9, 7, fifth_level)
    blur = lambda ref, i: fold(*[ref[pl.ds(2 * i + s - 2, 8, stride=2), :] for s in range(5)])
    for i in (2, 8, 11):
        e4[i : i + 8, :] = columns_strided(blur(e3, i), 1) * (1.0 / 256.0)
    e5[2:10, :] = columns_strided(blur(e4, 2), 2) * (1.0 / 256.0)

    def lanes_up(y, n):
        even = 0.125 * (right(y, n) + left(y, n)) + 0.75 * y
        odd = 0.5 * (right(y, n // 2) + left(y, n // 2))
        return even, odd

    def on_grid(y, n, parity):
        even, odd = lanes_up(y, n)
        return jnp.where(parity, odd, even)

    parity_four = (lane % 4) != 0
    parity_three = (lane % 2) != 0

    def coefficient_b(fine, coarse, guide, sums, start, n, parity):
        parts = []
        for i in range(start // 2, start // 2 + 4):
            made = [rows_up(coarse[i - 1, g], coarse[i, g], coarse[i + 1, g]) for g in range(2)]
            for odd in range(2):
                x = 2 * i + odd
                place = spread(guide, x) * 15.0
                terms = [
                    hat(place, channel[g]) * (fine[x, g] - 0.5 * on_grid(made[g][odd], n, parity)) for g in range(2)
                ]
                parts.append(terms[0] + terms[1])
        sums[start : start + 8, :] = eight_totals(parts)

    for start in (4, 12):
        coefficient_b(b4, b5, e4, c4, start, 4, parity_four)
    for start in (10, 18, 26):
        coefficient_b(b3, b4, e3, c3, start, 2, parity_three)

    def raise_rows(src, dst, start, count, index=()):
        above = src[index + (pl.ds(start - 1, count), slice(None))]
        here = src[index + (pl.ds(start, count), slice(None))]
        below = src[index + (pl.ds(start + 1, count), slice(None))]
        even, odd = rows_up(above, here, below)
        dst[index + (pl.ds(2 * start, count, stride=2), slice(None))] = 0.5 * even
        dst[index + (pl.ds(2 * start + 1, count, stride=2), slice(None))] = 0.5 * odd

    r5[...] = e5[...] * (1.0 - 0.5 * gains[4])
    raise_rows(r5, u4, 1, 8)
    for t in range(3):
        rows = slice(8 * t, 8 * t + 8)
        value = gains[4] * (0.5 * e4[rows, :] + c4[rows, :]) + on_grid(u4[rows, :], 4, parity_four)
        r4[rows, :] = value - (0.5 * gains[3]) * e4[rows, :]
    raise_rows(r4, u3, 4, 8)
    raise_rows(r4, u3, 8, 8)
    for t in range(1, 4):
        rows = slice(8 * t, 8 * t + 8)
        value = gains[3] * (0.5 * e3[rows, :] + c3[rows, :]) + on_grid(u3[rows, :], 2, parity_three)
        r3[rows, :] = value - (0.5 * gains[2]) * e3[rows, :]

    base_a = lane // 2 + 12
    column_s = jnp.where((lane // 32) % 2 == 0, lane % 32 - 24 + 256, lane % 32 + 120 + 256)
    base_s = column_s // 2 - 128 + 12
    odd_column = (lane % 2) != 0
    clip = lambda x: jnp.clip(x, 0, 127)
    base_a, base_s = clip(base_a), clip(base_s)

    def expand(y, at):
        even, odd = 0.125 * (right(y) + left(y)) + 0.75 * y, 0.5 * (y + left(y))
        return jnp.where(odd_column, pick(odd, at), pick(even, at))

    scale_two = 2.0 / (BETA * 2.0**16)

    def widen(i, carry):
        for g in range(2):
            wide3[i, g] = expand(b3[i, g], base_a)
        wide3[i, 2] = on_grid(s3[i, 0], 2, odd_column) * (1.0 / (BETA * 2.0**24))
        return carry

    loop(10, 32, 11, widen)

    def coefficient_two(t, carry):
        fine = [raised([wide3[4 * t + 10 + n, g] for n in range(6)]) for g in range(3)]
        parts, side = [], []
        for n in range(8):
            x = 8 * t + 22 + n
            place = spread(g2, 0, x) * 15.0
            terms = [hat(place, channel[g]) * (d2[x, g] * scale_two - fine[g][n]) for g in range(2)]
            parts.append(terms[0] + terms[1])
            place = spread(h2, 0, x) * 15.0
            side.append(hat(place, split) * (s2[x, 0] * scale_two - fine[2][n]))
        rows = pl.ds(8 * t + 22, 8)
        c2a[rows, :] = 0.5 * eight_totals(parts)
        both = eight_totals(side)
        c2s[rows, :] = 0.5 * (both + right(both, 64))
        return carry

    loop(0, 5, UNROLL_SUMS, coefficient_two)
    for start in (8, 16, 24):
        raise_rows(r3, w2, start, 8)
    for t in range(2, 8):
        rows = slice(8 * t, 8 * t + 8)
        coarse = w2[rows, :]
        value = gains[2] * (0.5 * g2[0, rows, :] + c2a[rows, :]) + expand(coarse, base_a)
        r2a[rows, :] = value - (0.5 * gains[1]) * g2[0, rows, :]
        guide = h2[0, rows, :]
        value = gains[2] * (0.5 * guide + c2s[rows, :]) + expand(coarse, base_s)
        r2s[rows, :] = value - (0.5 * gains[1]) * guide

    def side_one(t, carry):
        rows = [s2[4 * t + 22 + n, 0] for n in range(6)]
        fine = [raised(y) for y in ([right(y) for y in rows], rows, [left(y) for y in rows])]
        parts = [[], []]
        for n in range(8):
            ups = two_phases(*[f[n] for f in fine])
            for c in range(2):
                x = 8 * t + 46 + n
                parts[c].append(hat(spread(h1, c, x) * 15.0, split) * (s1[x, c] * 1024.0 - ups[c]))
        for c in range(2):
            both = eight_totals(parts[c])
            c1s[c, pl.ds(8 * t + 46, 8), :] = both + right(both, 64)
        return carry

    loop(0, 9, UNROLL_SUMS, side_one)

    def side_zero(t, carry):
        rows = [[s1[4 * t + 47 + n, c] for n in range(6)] for c in range(2)]
        fine = [raised(y) for y in ([right(y) for y in rows[1]], rows[0], rows[1], [left(y) for y in rows[0]])]
        parts = [[] for c in range(4)]
        for n in range(8):
            ups = four_phases(*[f[n] for f in fine])
            for c in range(4):
                place = spread(lum, c, 8 * t + 96 + n) * (15.0 / BETA)
                parts[c].append(hat(place, split) * ups[c])
        for c in range(4):
            both = eight_totals(parts[c])
            both = both + right(both, 64)
            sums_s[c, pl.ds(pl.multiple_of(8 * t, 8), 8), :] = both
        return carry

    loop(0, 16, UNROLL_SUMS, side_zero)
    scale_one = gains[1] * (1.0 / (BETA * 2.0**18))
    for start in (20, 28, 36, 44, 52):
        raise_rows(r2a, wide_a, start, 8)
        raise_rows(r2s, wide_s, start, 8)

    def collapse_one(t, carry):
        rows = pl.ds(pl.multiple_of(8 * t, 8), 8)
        y, z = wide_a[rows, :], wide_s[rows, :]
        m, y, p = edges_two(y, z)
        ups_a = two_phases(m, y, p)
        ups_s = two_phases(right(z), z, left(z))
        found = []
        for c in range(2):
            guide = g1[c, rows, :]
            found.append(
                (0.5 * (gains[1] - gains[0])) * guide + scale_one * c1a[c, rows, :] + 0.5 * ups_a[c]
            )
        side = []
        for c in range(2):
            guide = h1[c, rows, :]
            side.append((0.5 * (gains[1] - gains[0])) * guide + scale_one * c1s[c, rows, :] + 0.5 * ups_s[c])
        found = edges_one(found[0], found[1], side[0], side[1])
        for n in range(4):
            rest_in[n, rows, :] = found[n]
        return carry

    rest_in = lum
    loop(5, 15, 5, collapse_one)

    scale_zero = gains[0] * (1.0 / (BETA * 2.0**10))
    source = iota((256, 256), 0)
    target = iota((256, 256), 1)
    inverse = jnp.where(target == 4 * (source % 64) + source // 64, 1.0, 0.0).astype(jnp.bfloat16)

    def collapse_zero(t, carry):
        start = pl.multiple_of(8 * t, 8)
        fine = []
        for n in range(4):
            rows = [rest_in[n, pl.ds(start + 47 + k, 8), :] for k in range(3)]
            fine.append(rows_up(*rows))
        for odd in range(2):
            ups = four_phases(*[f[odd] for f in fine])
            for c in range(4):
                rest[c, pl.ds(2 * start + odd, 8, stride=2), :] = 0.25 * ups[c]
        for c in range(4):
            for k in range(2):
                rows = pl.ds(pl.multiple_of(2 * start, 16) + 8 * k, 8)
                total = ends(sums[c, rows, :], sums_s[c, rows, :], 0, 127)
                rest[c, rows, :] = rest[c, rows, :] - scale_zero * total
        return carry

    loop(0, 8, 4, collapse_zero)
    low_half = iota((128, LANES), 1) < 64
    halves = [[], []]
    for pair in range(2):
        a, b = rest[2 * pair], rest[2 * pair + 1]
        halves[0].append(jnp.where(low_half, a, right(b, 64)))
        halves[1].append(jnp.where(low_half, right(a, 64), b))
    both = jnp.concatenate([jnp.concatenate(h, axis=1) for h in halves], axis=0)
    natural = select_columns(both, inverse)
    out[:, :256] = natural[:128] + gains[0] * base_term[:, :256]
    out[:, 256:] = natural[128:] + gains[0] * base_term[:, 256:]


def shape(*dims):
    return jax.ShapeDtypeStruct(dims, F32)


def vmem(*dims):
    return pltpu.VMEM(dims, F32)


def run_a(top, mid, bottom):
    whole = pl.BlockSpec(memory_space=pltpu.VMEM)
    return pl.pallas_call(
        kernel_a,
        out_shape=(
            shape(160, 4, HALF, LANES),
            shape(80, 2, HALF, LANES),
            shape(40, 2, HALF, LANES),
            shape(4, 128, LANES),
            shape(2, 160, LANES),
            shape(1, 80, LANES),
            shape(40, LANES),
            shape(128, 512),
        ),
        in_specs=[whole] * 3,
        out_specs=(whole,) * 8,
        scratch_shapes=[vmem(4, ROWS, LANES)],
        compiler_params=pltpu.CompilerParams(vmem_limit_bytes=40 << 20),
        cost_estimate=pl.CostEstimate(flops=60_000_000, transcendentals=2_600_000, bytes_accessed=6_000_000),
    )(top, mid, bottom)


def run_c(d1, d2, x15, g1):
    whole = pl.BlockSpec(memory_space=pltpu.VMEM)
    return pl.pallas_call(
        kernel_c,
        out_shape=(shape(4, 128, LANES), shape(2, 160, LANES)),
        in_specs=[whole] * 4,
        out_specs=(whole, whole),
        compiler_params=pltpu.CompilerParams(vmem_limit_bytes=40 << 20),
        cost_estimate=pl.CostEstimate(flops=30_000_000, transcendentals=0, bytes_accessed=3_000_000),
    )(d1, d2, x15, g1)


def run_b(gain, *arrays):
    whole = pl.BlockSpec(memory_space=pltpu.VMEM)
    return pl.pallas_call(
        kernel_b,
        out_shape=shape(128, 512),
        in_specs=[pl.BlockSpec(memory_space=pltpu.SMEM)] + [whole] * len(arrays),
        out_specs=whole,
        scratch_shapes=[
            vmem(4, ROWS, LANES),
            vmem(160, 2, HALF, LANES),
            vmem(80, 1, HALF, LANES),
            vmem(40, 1, HALF, LANES),
            vmem(2, 160, LANES),
            vmem(1, 80, LANES),
            vmem(40, LANES),
            vmem(40, 2, HALF, LANES),
            vmem(24, 2, HALF, LANES),
            vmem(16, 2, HALF, LANES),
            vmem(40, LANES),
            vmem(24, LANES),
            vmem(16, LANES),
            vmem(24, LANES),
            vmem(40, LANES),
            vmem(80, LANES),
            vmem(80, LANES),
            vmem(2, 160, LANES),
            vmem(4, 128, LANES),
            vmem(16, LANES),
            vmem(24, LANES),
            vmem(24, LANES),
            vmem(40, LANES),
            vmem(40, LANES),
            vmem(40, 3, HALF, LANES),
            vmem(80, LANES),
            vmem(80, LANES),
            vmem(80, LANES),
            vmem(160, LANES),
            vmem(160, LANES),
            vmem(4, 128, LANES),
        ],
        compiler_params=pltpu.CompilerParams(vmem_limit_bytes=48 << 20),
        cost_estimate=pl.CostEstimate(flops=60_000_000, transcendentals=1_300_000, bytes_accessed=6_000_000),
    )(gain, *arrays)


def ring(axis, shift):
    count = lax.axis_size(axis)
    return [(i, (i + shift) % count) for i in range(count)]


def local(luminance, level_gain):
    down = lambda x: lax.ppermute(x, "row", ring("row", 1))
    up = lambda x: lax.ppermute(x, "row", ring("row", -1))
    top, bottom = down(luminance), up(luminance)
    far_left = lax.ppermute(luminance[:, 384:], "col", ring("col", 1))
    far_right = lax.ppermute(luminance[:, :LANES], "col", ring("col", -1))
    d1, d2, d3, x15, g1, g2, g3, base_term = run_a(top, luminance, bottom)
    far_left, far_right, d3 = lax.optimization_barrier((far_left, far_right, d3))
    far = jnp.concatenate([far_left, far_right], axis=1)
    far_top, far_bottom = down(far[32:]), up(far[:96])
    sums, c1a = run_c(d1, d2, x15, g1)
    return run_b(
        level_gain, top, luminance, bottom, far_left, far_right, far_top, far_bottom,
        d2, d3, g1, g2, g3, base_term, sums, c1a,
    )


def solution(mesh):
    return jax.shard_map(
        local, mesh=mesh, in_specs=(P("row", "col"), P()), out_specs=P("row", "col"), check_vma=False
    )
```

```python
import math

import jax
import jax.numpy as jnp
from jax import lax
from jax.experimental import pallas as pl
from jax.experimental.pallas import tpu as pltpu
from jax.sharding import PartitionSpec as P


ROWS = 320
LANES = 128
HALF = 8
STEP = 1.0 / 15.0
BETA = math.sqrt(800.0 * math.log2(math.e))
F32 = jnp.float32
UNROLL_TWO = {1: 77, 2: 39}
UNROLL_SUMS = 8


def iota(shape, dim):
    return lax.broadcasted_iota(jnp.int32, shape, dim)


def left(x, n=1):
    return pltpu.roll(x, LANES - n, axis=x.ndim - 1)


def right(x, n=1):
    return pltpu.roll(x, n, axis=x.ndim - 1)


def pick(x, idx):
    return jnp.take_along_axis(x, idx, axis=1)


def select_columns(x, table):
    hi = x.astype(jnp.bfloat16)
    rest = x - hi.astype(F32)
    mid = rest.astype(jnp.bfloat16)
    low = (rest - mid.astype(F32)).astype(jnp.bfloat16)
    count = x.shape[0]
    out = jnp.dot(jnp.concatenate([hi, mid, low], axis=0), table, preferred_element_type=F32)
    return out[:count] + out[count : 2 * count] + out[2 * count :]


def spread(ref, *index):
    return ref[index[:-1] + (pl.ds(index[-1], HALF, stride=0), slice(None))]


def fold(y0, y1, y2, y3, y4):
    return (y0 + y4) + 6.0 * y2 + 4.0 * (y1 + y3)


def bump(lum, anchor, power):
    u = lum - anchor
    return u * jnp.exp2(power - u * u)


def columns_from_four(y):
    y0, y1, y2, y3 = y
    return (
        (right(y2) + y2) + 6.0 * y0 + (right(y3) + y1),
        (y0 + left(y0)) + 6.0 * y2 + (y1 + y3),
    )


def columns_from_two(y):
    y0, y1 = y
    return fold(right(y0), right(y1), y0, y1, left(y0))


def columns_strided(y, n):
    return fold(right(y, 2 * n), right(y, n), y, left(y, n), left(y, 2 * n))


def loop(low, high, size, body, state=()):
    whole = (high - low) // size

    def several(t, state):
        for n in range(size):
            state = body(low + size * t + n, state)
        return state

    state = lax.fori_loop(0, whole, several, state)
    for i in range(low + size * whole, high):
        state = body(i, state)
    return state


def first_level(lum, anchors, d1, low, high, size, above=0):
    groups = len(anchors)

    def row(e, odd):
        values = [spread(lum, c, e - above) for c in range(4)]
        return [[bump(v, a, 2.0 * odd + 2.0 * (c % 2)) for c, v in enumerate(values)] for a in anchors]

    def step(i, state):
        even_before, even, odd_before = state
        odd = row(2 * i + 1, 1)
        even_next = row(2 * i + 2, 0)
        for g in range(groups):
            y = [
                (even_before[g][c] + even_next[g][c]) + 6.0 * even[g][c] + (odd_before[g][c] + odd[g][c])
                for c in range(4)
            ]
            out = columns_from_four(y)
            d1[i, 2 * g] = out[0]
            d1[i, 2 * g + 1] = out[1]
        return even, even_next, odd

    loop(low, high, size, step, (row(2 * low - 2, 0), row(2 * low, 0), row(2 * low - 1, 1)))


def next_levels(d1, d2, d3, groups):
    def second_level(i, carry):
        for g in range(groups):
            y = [fold(*[d1[2 * i + s - 2, 2 * g + c] for s in range(5)]) for c in range(2)]
            d2[i, g] = columns_from_two(y)
        return carry

    loop(2, 79, UNROLL_TWO[groups], second_level)

    def third_level(i, carry):
        for g in range(groups):
            d3[i, g] = columns_strided(fold(*[d2[2 * i + s - 2, g] for s in range(5)]), 1)
        return carry

    loop(2, 39, UNROLL_TWO[groups], third_level)


def rows_blurred(ref, c, base, count):
    return fold(*[ref[c, pl.ds(base + s - 2, count, stride=2), :] for s in range(5)])


def guide_chain(lum, scale, g1, g2, g3):
    def first(t, carry):
        i = pl.multiple_of(8 * t, 8) + 8
        y = [rows_blurred(lum, c, 2 * i, 8) * (1.0 + 3.0 * (c % 2)) for c in range(4)]
        out = columns_from_four(y)
        g1[0, pl.ds(i, 8), :] = out[0] * (scale / 256.0)
        g1[1, pl.ds(i, 8), :] = out[1] * (scale / 256.0)
        return carry

    loop(0, 18, 6, first)
    for i in (1, 151):
        y = [rows_blurred(lum, c, 2 * i, 8) * (1.0 + 3.0 * (c % 2)) for c in range(4)]
        out = columns_from_four(y)
        g1[0, i : i + 8, :] = out[0] * (scale / 256.0)
        g1[1, i : i + 8, :] = out[1] * (scale / 256.0)
    for i in (2, 8, 16, 24, 32, 40, 48, 56, 64, 71):
        y = [rows_blurred(g1, c, 2 * i, 8) for c in range(2)]
        g2[0, i : i + 8, :] = columns_from_two(y) * (1.0 / 256.0)
    for i in (2, 8, 16, 24, 31):
        g3[i : i + 8, :] = columns_strided(rows_blurred(g2, 0, 2 * i, 8), 1) * (1.0 / 256.0)


def anchor_tile(base):
    return (iota((HALF, LANES), 0) + base).astype(F32)


def phase_table():
    source = iota((256, 256), 0)
    target = iota((256, 256), 1)
    return jnp.where(source == 4 * (target % 64) + target // 64, 1.0, 0.0).astype(jnp.bfloat16)


def phases_of(block, table):
    count = block.shape[0]
    split = select_columns(jnp.concatenate([block[:, :256], block[:, 256:]], axis=0), table)
    low_half = iota((count, LANES), 1) < 64
    found = []
    for pair in range(2):
        a = split[:count, pair * LANES : (pair + 1) * LANES]
        b = split[count:, pair * LANES : (pair + 1) * LANES]
        found += [jnp.where(low_half, a, right(b, 64)), jnp.where(low_half, right(a, 64), b)]
    return found


def hat(place, channel):
    return jnp.maximum(0.0, 1.0 - jnp.abs(place - channel))


def eight_totals(parts):
    sublane = iota((HALF, LANES), 0)

    def join(a, b, offset, span):
        mine = (sublane - offset + HALF) % (2 * span) < span
        return jnp.where(mine, a, b) + pltpu.roll(jnp.where(mine, b, a), HALF - span, axis=0)

    def four(a, b, c, d, offset):
        return join(join(a, b, offset, 4), join(c, d, offset + 2, 4), offset, 2)

    x = parts
    return join(four(x[0], x[4], x[2], x[6], 0), four(x[1], x[5], x[3], x[7], 1), 0, 1)


def rows_up(before, here, after):
    later = here + after
    return here + 0.25 * ((before + here) + later), later


def raised(rows):
    sums = [a + b for a, b in zip(rows, rows[1:])]
    out = []
    for n in range(1, len(rows) - 1):
        out += [rows[n] + 0.25 * (sums[n - 1] + sums[n]), sums[n]]
    return out


def two_phases(m, y, p):
    return y + 0.25 * ((m + y) + (y + p)), y + p


def four_phases(m, q0, q1, p):
    t0, t1, tm = q0 + q1, q1 + p, m + q0
    return q0 + 0.25 * (tm + t0), t0, q1 + 0.25 * (t0 + t1), t1


def sums_of_level_zero(d1, x15, sums):
    channel = [anchor_tile(HALF * g) for g in range(2)]

    def level_zero(t, carry):
        parts = [[None] * 8 for c in range(4)]
        for g in range(2):
            rows = [[d1[4 * t + 47 + n, 2 * g + c] for n in range(6)] for c in range(2)]
            fine = [raised(y) for y in ([right(y) for y in rows[1]], rows[0], rows[1], [left(y) for y in rows[0]])]
            for n in range(8):
                ups = four_phases(*[f[n] for f in fine])
                for c in range(4):
                    part = hat(spread(x15, c, 8 * t + n), channel[g]) * ups[c]
                    parts[c][n] = part if g == 0 else parts[c][n] + part
        for c in range(4):
            sums[c, pl.ds(8 * t, 8), :] = eight_totals(parts[c])
        return carry

    return level_zero


def sums_in_a(d1, d2, x15, g1, sums, c1a):
    channel = [anchor_tile(HALF * g) for g in range(2)]

    def level_one(t, carry):
        parts = [[None] * 8 for c in range(2)]
        for g in range(2):
            rows = [d2[4 * t + 22 + n, g] for n in range(6)]
            fine = [raised(y) for y in ([right(y) for y in rows], rows, [left(y) for y in rows])]
            for n in range(8):
                ups = two_phases(*[f[n] for f in fine])
                for c in range(2):
                    x = 8 * t + 46 + n
                    part = hat(spread(g1, c, x) * 15.0, channel[g]) * (d1[x, 2 * g + c] * 1024.0 - ups[c])
                    parts[c][n] = part if g == 0 else parts[c][n] + part
        for c in range(2):
            c1a[c, pl.ds(8 * t + 46, 8), :] = eight_totals(parts[c])
        return carry

    loop(0, 9, UNROLL_SUMS, level_one)

    level_zero = sums_of_level_zero(d1, x15, sums)
    level_zero(0, ())
    level_zero(15, ())


def kernel_z(mid, x15, base_term, near_left, near_right, d1, sums, lum):
    for c, part in enumerate(phases_of(mid[...], phase_table())):
        x15[c] = part * 15.0
        lum[c] = part * BETA
    near_left[...] = mid[:, :LANES]
    near_right[...] = mid[:, 384:]

    def natural(t, carry):
        rows = pl.ds(pl.multiple_of(8 * t, 8), 8)
        value = mid[rows, :]
        place = value * 15.0
        lower = jnp.floor(place)
        part = place - lower
        near = value - lower * STEP
        far = value - (lower + 1.0) * STEP
        bend = (1.0 - part) * near * jnp.exp(near * near * -800.0) + part * far * jnp.exp(far * far * -800.0)
        base_term[rows, :] = 0.5 * value + bend
        return carry

    loop(0, 16, 8, natural)
    anchors = [anchor_tile(HALF * g) * (BETA * STEP) for g in range(2)]
    first_level(lum, anchors, d1, 49, 111, 31, above=96)
    loop(1, 15, 7, sums_of_level_zero(d1, x15, sums))


def kernel_a(top, bottom, x15, d1_in, sums_in, d1, d2, d3, g1, g2, g3, sums, c1a, lum):
    table = phase_table()
    for ref, skip, start in ((top, 32, 0), (bottom, 0, 224)):
        for c, part in enumerate(phases_of(ref[skip : skip + 96, :], table)):
            lum[c, start : start + 96, :] = part * BETA
    for c in range(4):
        lum[c, 96:224, :] = x15[c] * (BETA * STEP)
    guide_chain(lum, 1.0 / BETA, g1, g2, g3)
    anchors = [anchor_tile(HALF * g) * (BETA * STEP) for g in range(2)]
    first_level(lum, anchors, d1, 2, 49, 24)
    first_level(lum, anchors, d1, 111, 159, 24)
    next_levels(d1, d2, d3, 2)
    sums_in_a(d1, d2, x15, g1, sums, c1a)


def kernel_b(
    gain_ref, far_left, near_left, near_right, far_right,
    d2, d3, g1, g2, g3, base_term, sums, c1a, out,
    lum, s1, s2, s3, h1, h2, h3, b3, b4, b5, e3, e4, e5,
    c4, c3, c2a, c2s, c1s, sums_s, r5, r4, u4, r3, u3, wide3, w2, r2a, r2s, wide_a, wide_s, rest,
):
    gains = [gain_ref[i] for i in range(5)]
    lane = iota((HALF, LANES), 1)
    channel = [anchor_tile(HALF * g) for g in range(2)]
    split = anchor_tile(0) + jnp.where(lane >= 64, 8.0, 0.0)

    source = iota((512, 256), 0)
    target = iota((512, 256), 1)
    wanted = 32 + 320 * ((target // 32) % 2) + 4 * (target % 32) + target // 64
    table = jnp.where(source == wanted, 1.0, 0.0).astype(jnp.bfloat16)
    count = 160
    for start in range(0, ROWS, count):
        part = slice(start, start + count)
        natural = [ref[part, :] for ref in (far_left, near_left, near_right, far_right)]
        pieces = select_columns(jnp.concatenate(natural, axis=1), table)
        low_half = iota((count, LANES), 1) < 64
        for pair in range(2):
            a = pieces[:, pair * LANES : (pair + 1) * LANES] * BETA
            b = right(a, 64)
            lum[2 * pair, start : start + count, :] = jnp.where(low_half, a, b)
            lum[2 * pair + 1, start : start + count, :] = jnp.where(low_half, b, a)
    guide_chain(lum, 1.0 / BETA, h1, h2, h3)
    first_level(lum, [split * (BETA * STEP)], s1, 2, 159, 53)
    next_levels(s1, s2, s3, 1)

    first, last = lane == 0, lane == 127
    turn = lambda x, source, to: pltpu.roll(x, (to - source) % LANES, axis=1)

    def ends(x, t, low, high):
        return jnp.where(lane >= high, turn(t, 39, 127), jnp.where(lane <= low, turn(t, 24, 0), x))

    def edges_one(q0, q1, t0, t1):
        q0, q1 = ends(q0, t0, 2, 126), ends(q1, t1, 2, 126)
        return jnp.where(first, turn(t1, 23, 0), right(q1)), q0, q1, jnp.where(last, turn(t0, 40, 127), left(q0))

    def edges_two(y, t):
        y = ends(y, t, 1, 127)
        return jnp.where(first, turn(t, 23, 0), right(y)), y, jnp.where(last, turn(t, 40, 127), left(y))

    from_a = (lane >= 14) & (lane <= 74)
    index_a = jnp.clip(2 * (lane - 12), 0, 127)
    index_s = [jnp.clip(64 * g + jnp.where(lane < 14, 2 * lane, 2 * lane - 112), 0, 127) for g in range(2)]

    def merge(i, carry):
        for g in range(2):
            b3[i, g] = jnp.where(from_a, pick(d3[i, g], index_a), pick(s3[i, 0], index_s[g])) * (
                1.0 / (BETA * 2.0**24)
            )
        return carry

    loop(2, 39, 8, merge)
    for t in range(5):
        rows = slice(8 * t, 8 * t + 8)
        e3[rows, :] = jnp.where(from_a, pick(g3[rows, :], index_a), pick(h3[rows, :], index_s[0]))

    def fourth_level(i, carry):
        for g in range(2):
            b4[i, g] = columns_strided(fold(*[b3[2 * i + s - 2, g] for s in range(5)]), 1) * (1.0 / 256.0)
        return carry

    loop(2, 19, 17, fourth_level)

    def fifth_level(i, carry):
        for g in range(2):
            b5[i, g] = columns_strided(fold(*[b4[2 * i + s - 2, g] for s in range(5)]), 2) * (1.0 / 256.0)
        return carry

    loop(2, 9, 7, fifth_level)
    blur = lambda ref, i: fold(*[ref[pl.ds(2 * i + s - 2, 8, stride=2), :] for s in range(5)])
    for i in (2, 8, 11):
        e4[i : i + 8, :] = columns_strided(blur(e3, i), 1) * (1.0 / 256.0)
    e5[2:10, :] = columns_strided(blur(e4, 2), 2) * (1.0 / 256.0)

    def lanes_up(y, n):
        even = 0.125 * (right(y, n) + left(y, n)) + 0.75 * y
        odd = 0.5 * (right(y, n // 2) + left(y, n // 2))
        return even, odd

    def on_grid(y, n, parity):
        even, odd = lanes_up(y, n)
        return jnp.where(parity, odd, even)

    parity_four = (lane % 4) != 0
    parity_three = (lane % 2) != 0

    def coefficient_b(fine, coarse, guide, sums, start, n, parity):
        parts = []
        for i in range(start // 2, start // 2 + 4):
            made = [rows_up(coarse[i - 1, g], coarse[i, g], coarse[i + 1, g]) for g in range(2)]
            for odd in range(2):
                x = 2 * i + odd
                place = spread(guide, x) * 15.0
                terms = [
                    hat(place, channel[g]) * (fine[x, g] - 0.5 * on_grid(made[g][odd], n, parity)) for g in range(2)
                ]
                parts.append(terms[0] + terms[1])
        sums[start : start + 8, :] = eight_totals(parts)

    for start in (4, 12):
        coefficient_b(b4, b5, e4, c4, start, 4, parity_four)
    for start in (10, 18, 26):
        coefficient_b(b3, b4, e3, c3, start, 2, parity_three)

    def raise_rows(src, dst, start, count, index=()):
        above = src[index + (pl.ds(start - 1, count), slice(None))]
        here = src[index + (pl.ds(start, count), slice(None))]
        below = src[index + (pl.ds(start + 1, count), slice(None))]
        even, odd = rows_up(above, here, below)
        dst[index + (pl.ds(2 * start, count, stride=2), slice(None))] = 0.5 * even
        dst[index + (pl.ds(2 * start + 1, count, stride=2), slice(None))] = 0.5 * odd

    r5[...] = e5[...] * (1.0 - 0.5 * gains[4])
    raise_rows(r5, u4, 1, 8)
    for t in range(3):
        rows = slice(8 * t, 8 * t + 8)
        value = gains[4] * (0.5 * e4[rows, :] + c4[rows, :]) + on_grid(u4[rows, :], 4, parity_four)
        r4[rows, :] = value - (0.5 * gains[3]) * e4[rows, :]
    raise_rows(r4, u3, 4, 8)
    raise_rows(r4, u3, 8, 8)
    for t in range(1, 4):
        rows = slice(8 * t, 8 * t + 8)
        value = gains[3] * (0.5 * e3[rows, :] + c3[rows, :]) + on_grid(u3[rows, :], 2, parity_three)
        r3[rows, :] = value - (0.5 * gains[2]) * e3[rows, :]

    base_a = lane // 2 + 12
    column_s = jnp.where((lane // 32) % 2 == 0, lane % 32 - 24 + 256, lane % 32 + 120 + 256)
    base_s = column_s // 2 - 128 + 12
    odd_column = (lane % 2) != 0
    clip = lambda x: jnp.clip(x, 0, 127)
    base_a, base_s = clip(base_a), clip(base_s)

    def expand(y, at):
        even, odd = 0.125 * (right(y) + left(y)) + 0.75 * y, 0.5 * (y + left(y))
        return jnp.where(odd_column, pick(odd, at), pick(even, at))

    scale_two = 2.0 / (BETA * 2.0**16)

    def widen(i, carry):
        for g in range(2):
            wide3[i, g] = expand(b3[i, g], base_a)
        wide3[i, 2] = on_grid(s3[i, 0], 2, odd_column) * (1.0 / (BETA * 2.0**24))
        return carry

    loop(10, 32, 11, widen)

    def coefficient_two(t, carry):
        fine = [raised([wide3[4 * t + 10 + n, g] for n in range(6)]) for g in range(3)]
        parts, side = [], []
        for n in range(8):
            x = 8 * t + 22 + n
            place = spread(g2, 0, x) * 15.0
            terms = [hat(place, channel[g]) * (d2[x, g] * scale_two - fine[g][n]) for g in range(2)]
            parts.append(terms[0] + terms[1])
            place = spread(h2, 0, x) * 15.0
            side.append(hat(place, split) * (s2[x, 0] * scale_two - fine[2][n]))
        rows = pl.ds(8 * t + 22, 8)
        c2a[rows, :] = 0.5 * eight_totals(parts)
        both = eight_totals(side)
        c2s[rows, :] = 0.5 * (both + right(both, 64))
        return carry

    loop(0, 5, UNROLL_SUMS, coefficient_two)
    for start in (8, 16, 24):
        raise_rows(r3, w2, start, 8)
    for t in range(2, 8):
        rows = slice(8 * t, 8 * t + 8)
        coarse = w2[rows, :]
        value = gains[2] * (0.5 * g2[0, rows, :] + c2a[rows, :]) + expand(coarse, base_a)
        r2a[rows, :] = value - (0.5 * gains[1]) * g2[0, rows, :]
        guide = h2[0, rows, :]
        value = gains[2] * (0.5 * guide + c2s[rows, :]) + expand(coarse, base_s)
        r2s[rows, :] = value - (0.5 * gains[1]) * guide

    def side_one(t, carry):
        rows = [s2[4 * t + 22 + n, 0] for n in range(6)]
        fine = [raised(y) for y in ([right(y) for y in rows], rows, [left(y) for y in rows])]
        parts = [[], []]
        for n in range(8):
            ups = two_phases(*[f[n] for f in fine])
            for c in range(2):
                x = 8 * t + 46 + n
                parts[c].append(hat(spread(h1, c, x) * 15.0, split) * (s1[x, c] * 1024.0 - ups[c]))
        for c in range(2):
            both = eight_totals(parts[c])
            c1s[c, pl.ds(8 * t + 46, 8), :] = both + right(both, 64)
        return carry

    loop(0, 9, UNROLL_SUMS, side_one)

    def side_zero(t, carry):
        rows = [[s1[4 * t + 47 + n, c] for n in range(6)] for c in range(2)]
        fine = [raised(y) for y in ([right(y) for y in rows[1]], rows[0], rows[1], [left(y) for y in rows[0]])]
        parts = [[] for c in range(4)]
        for n in range(8):
            ups = four_phases(*[f[n] for f in fine])
            for c in range(4):
                place = spread(lum, c, 8 * t + 96 + n) * (15.0 / BETA)
                parts[c].append(hat(place, split) * ups[c])
        for c in range(4):
            both = eight_totals(parts[c])
            both = both + right(both, 64)
            sums_s[c, pl.ds(pl.multiple_of(8 * t, 8), 8), :] = both
        return carry

    loop(0, 16, UNROLL_SUMS, side_zero)
    scale_one = gains[1] * (1.0 / (BETA * 2.0**18))
    for start in (20, 28, 36, 44, 52):
        raise_rows(r2a, wide_a, start, 8)
        raise_rows(r2s, wide_s, start, 8)

    def collapse_one(t, carry):
        rows = pl.ds(pl.multiple_of(8 * t, 8), 8)
        y, z = wide_a[rows, :], wide_s[rows, :]
        m, y, p = edges_two(y, z)
        ups_a = two_phases(m, y, p)
        ups_s = two_phases(right(z), z, left(z))
        found = []
        for c in range(2):
            guide = g1[c, rows, :]
            found.append(
                (0.5 * (gains[1] - gains[0])) * guide + scale_one * c1a[c, rows, :] + 0.5 * ups_a[c]
            )
        side = []
        for c in range(2):
            guide = h1[c, rows, :]
            side.append((0.5 * (gains[1] - gains[0])) * guide + scale_one * c1s[c, rows, :] + 0.5 * ups_s[c])
        found = edges_one(found[0], found[1], side[0], side[1])
        for n in range(4):
            rest_in[n, rows, :] = found[n]
        return carry

    rest_in = lum
    loop(5, 15, 5, collapse_one)

    scale_zero = gains[0] * (1.0 / (BETA * 2.0**10))
    source = iota((256, 256), 0)
    target = iota((256, 256), 1)
    inverse = jnp.where(target == 4 * (source % 64) + source // 64, 1.0, 0.0).astype(jnp.bfloat16)

    def collapse_zero(t, carry):
        start = pl.multiple_of(8 * t, 8)
        fine = []
        for n in range(4):
            rows = [rest_in[n, pl.ds(start + 47 + k, 8), :] for k in range(3)]
            fine.append(rows_up(*rows))
        for odd in range(2):
            ups = four_phases(*[f[odd] for f in fine])
            for c in range(4):
                rest[c, pl.ds(2 * start + odd, 8, stride=2), :] = 0.25 * ups[c]
        for c in range(4):
            for k in range(2):
                rows = pl.ds(pl.multiple_of(2 * start, 16) + 8 * k, 8)
                total = ends(sums[c, rows, :], sums_s[c, rows, :], 0, 127)
                rest[c, rows, :] = rest[c, rows, :] - scale_zero * total
        return carry

    loop(0, 8, 4, collapse_zero)
    low_half = iota((128, LANES), 1) < 64
    halves = [[], []]
    for pair in range(2):
        a, b = rest[2 * pair], rest[2 * pair + 1]
        halves[0].append(jnp.where(low_half, a, right(b, 64)))
        halves[1].append(jnp.where(low_half, right(a, 64), b))
    both = jnp.concatenate([jnp.concatenate(h, axis=1) for h in halves], axis=0)
    natural = select_columns(both, inverse)
    out[:, :256] = natural[:128] + gains[0] * base_term[:, :256]
    out[:, 256:] = natural[128:] + gains[0] * base_term[:, 256:]


def shape(*dims):
    return jax.ShapeDtypeStruct(dims, F32)


def vmem(*dims):
    return pltpu.VMEM(dims, F32)


def run_z(mid):
    whole = pl.BlockSpec(memory_space=pltpu.VMEM)
    return pl.pallas_call(
        kernel_z,
        out_shape=(
            shape(4, 128, LANES),
            shape(128, 512),
            shape(128, LANES),
            shape(128, LANES),
            shape(160, 4, HALF, LANES),
            shape(4, 128, LANES),
        ),
        in_specs=[whole],
        out_specs=(whole,) * 6,
        scratch_shapes=[vmem(4, 128, LANES)],
        compiler_params=pltpu.CompilerParams(vmem_limit_bytes=40 << 20),
        cost_estimate=pl.CostEstimate(flops=30_000_000, transcendentals=1_100_000, bytes_accessed=2_000_000),
    )(mid)


def run_a(top, bottom, x15, d1, sums):
    whole = pl.BlockSpec(memory_space=pltpu.VMEM)
    return pl.pallas_call(
        kernel_a,
        out_shape=(
            shape(160, 4, HALF, LANES),
            shape(80, 2, HALF, LANES),
            shape(40, 2, HALF, LANES),
            shape(2, 160, LANES),
            shape(1, 80, LANES),
            shape(40, LANES),
            shape(4, 128, LANES),
            shape(2, 160, LANES),
        ),
        in_specs=[whole] * 5,
        out_specs=(whole,) * 8,
        input_output_aliases={3: 0, 4: 6},
        scratch_shapes=[vmem(4, ROWS, LANES)],
        compiler_params=pltpu.CompilerParams(vmem_limit_bytes=40 << 20),
        cost_estimate=pl.CostEstimate(flops=60_000_000, transcendentals=2_600_000, bytes_accessed=6_000_000),
    )(top, bottom, x15, d1, sums)


def run_b(gain, *arrays):
    whole = pl.BlockSpec(memory_space=pltpu.VMEM)
    return pl.pallas_call(
        kernel_b,
        out_shape=shape(128, 512),
        in_specs=[pl.BlockSpec(memory_space=pltpu.SMEM)] + [whole] * len(arrays),
        out_specs=whole,
        scratch_shapes=[
            vmem(4, ROWS, LANES),
            vmem(160, 2, HALF, LANES),
            vmem(80, 1, HALF, LANES),
            vmem(40, 1, HALF, LANES),
            vmem(2, 160, LANES),
            vmem(1, 80, LANES),
            vmem(40, LANES),
            vmem(40, 2, HALF, LANES),
            vmem(24, 2, HALF, LANES),
            vmem(16, 2, HALF, LANES),
            vmem(40, LANES),
            vmem(24, LANES),
            vmem(16, LANES),
            vmem(24, LANES),
            vmem(40, LANES),
            vmem(80, LANES),
            vmem(80, LANES),
            vmem(2, 160, LANES),
            vmem(4, 128, LANES),
            vmem(16, LANES),
            vmem(24, LANES),
            vmem(24, LANES),
            vmem(40, LANES),
            vmem(40, LANES),
            vmem(40, 3, HALF, LANES),
            vmem(80, LANES),
            vmem(80, LANES),
            vmem(80, LANES),
            vmem(160, LANES),
            vmem(160, LANES),
            vmem(4, 128, LANES),
        ],
        compiler_params=pltpu.CompilerParams(vmem_limit_bytes=48 << 20),
        cost_estimate=pl.CostEstimate(flops=60_000_000, transcendentals=1_300_000, bytes_accessed=6_000_000),
    )(gain, *arrays)


def ring(axis, shift):
    count = lax.axis_size(axis)
    return [(i, (i + shift) % count) for i in range(count)]


def local(luminance, level_gain):
    top = lax.ppermute(luminance, "row", ring("row", 1))
    bottom = lax.ppermute(luminance, "row", ring("row", -1))
    x15, base_term, mid_left, mid_right, d1, sums = run_z(luminance)
    near_left = jnp.concatenate([top[32:, :LANES], mid_left, bottom[:96, :LANES]], axis=0)
    near_right = jnp.concatenate([top[32:, 384:], mid_right, bottom[:96, 384:]], axis=0)
    far_left = lax.ppermute(near_right, "col", ring("col", 1))
    far_right = lax.ppermute(near_left, "col", ring("col", -1))
    d1, d2, d3, g1, g2, g3, sums, c1a = run_a(top, bottom, x15, d1, sums)
    return run_b(
        level_gain, far_left, near_left, near_right, far_right, d2, d3, g1, g2, g3, base_term, sums, c1a
    )


def solution(mesh):
    return jax.shard_map(
        local, mesh=mesh, in_specs=(P("row", "col"), P()), out_specs=P("row", "col"), check_vma=False
    )
```

```python
import math

import jax
import jax.numpy as jnp
from jax import lax
from jax.experimental import pallas as pl
from jax.experimental.pallas import tpu as pltpu
from jax.sharding import PartitionSpec as P


ROWS = 320
LANES = 128
HALF = 8
STEP = 1.0 / 15.0
BETA = math.sqrt(800.0 * math.log2(math.e))
F32 = jnp.float32
UNROLL_TWO = {1: 77, 2: 39}
UNROLL_SUMS = 8
EARLY = 28


def iota(shape, dim):
    return lax.broadcasted_iota(jnp.int32, shape, dim)


def left(x, n=1):
    return pltpu.roll(x, LANES - n, axis=x.ndim - 1)


def right(x, n=1):
    return pltpu.roll(x, n, axis=x.ndim - 1)


def pick(x, idx):
    return jnp.take_along_axis(x, idx, axis=1)


def select_columns(x, table):
    hi = x.astype(jnp.bfloat16)
    rest = x - hi.astype(F32)
    mid = rest.astype(jnp.bfloat16)
    low = (rest - mid.astype(F32)).astype(jnp.bfloat16)
    count = x.shape[0]
    out = jnp.dot(jnp.concatenate([hi, mid, low], axis=0), table, preferred_element_type=F32)
    return out[:count] + out[count : 2 * count] + out[2 * count :]


def spread(ref, *index):
    return ref[index[:-1] + (pl.ds(index[-1], HALF, stride=0), slice(None))]


def fold(y0, y1, y2, y3, y4):
    return (y0 + y4) + 6.0 * y2 + 4.0 * (y1 + y3)


def bump(lum, anchor, power):
    u = lum - anchor
    return u * jnp.exp2(power - u * u)


def columns_from_four(y):
    y0, y1, y2, y3 = y
    return (
        (right(y2) + y2) + 6.0 * y0 + (right(y3) + y1),
        (y0 + left(y0)) + 6.0 * y2 + (y1 + y3),
    )


def columns_from_two(y):
    y0, y1 = y
    return fold(right(y0), right(y1), y0, y1, left(y0))


def columns_strided(y, n):
    return fold(right(y, 2 * n), right(y, n), y, left(y, n), left(y, 2 * n))


def loop(low, high, size, body, state=()):
    whole = (high - low) // size

    def several(t, state):
        for n in range(size):
            state = body(low + size * t + n, state)
        return state

    state = lax.fori_loop(0, whole, several, state)
    for i in range(low + size * whole, high):
        state = body(i, state)
    return state


def first_level(lum, anchors, d1, low, high, size, above=0):
    groups = len(anchors)

    def row(e, odd):
        values = [spread(lum, c, e - above) for c in range(4)]
        return [[bump(v, a, 2.0 * odd + 2.0 * (c % 2)) for c, v in enumerate(values)] for a in anchors]

    def step(i, state):
        even_before, even, odd_before = state
        odd = row(2 * i + 1, 1)
        even_next = row(2 * i + 2, 0)
        for g in range(groups):
            y = [
                (even_before[g][c] + even_next[g][c]) + 6.0 * even[g][c] + (odd_before[g][c] + odd[g][c])
                for c in range(4)
            ]
            out = columns_from_four(y)
            d1[i, 2 * g] = out[0]
            d1[i, 2 * g + 1] = out[1]
        return even, even_next, odd

    loop(low, high, size, step, (row(2 * low - 2, 0), row(2 * low, 0), row(2 * low - 1, 1)))


def next_levels(d1, d2, d3, groups):
    def second_level(i, carry):
        for g in range(groups):
            y = [fold(*[d1[2 * i + s - 2, 2 * g + c] for s in range(5)]) for c in range(2)]
            d2[i, g] = columns_from_two(y)
        return carry

    loop(2, 79, UNROLL_TWO[groups], second_level)

    def third_level(i, carry):
        for g in range(groups):
            d3[i, g] = columns_strided(fold(*[d2[2 * i + s - 2, g] for s in range(5)]), 1)
        return carry

    loop(2, 39, UNROLL_TWO[groups], third_level)


def rows_blurred(ref, c, base, count):
    return fold(*[ref[c, pl.ds(base + s - 2, count, stride=2), :] for s in range(5)])


def guide_chain(lum, scale, g1, g2, g3):
    def first(t, carry):
        i = pl.multiple_of(8 * t, 8) + 8
        y = [rows_blurred(lum, c, 2 * i, 8) * (1.0 + 3.0 * (c % 2)) for c in range(4)]
        out = columns_from_four(y)
        g1[0, pl.ds(i, 8), :] = out[0] * (scale / 256.0)
        g1[1, pl.ds(i, 8), :] = out[1] * (scale / 256.0)
        return carry

    loop(0, 18, 6, first)
    for i in (1, 151):
        y = [rows_blurred(lum, c, 2 * i, 8) * (1.0 + 3.0 * (c % 2)) for c in range(4)]
        out = columns_from_four(y)
        g1[0, i : i + 8, :] = out[0] * (scale / 256.0)
        g1[1, i : i + 8, :] = out[1] * (scale / 256.0)
    for i in (2, 8, 16, 24, 32, 40, 48, 56, 64, 71):
        y = [rows_blurred(g1, c, 2 * i, 8) for c in range(2)]
        g2[0, i : i + 8, :] = columns_from_two(y) * (1.0 / 256.0)
    for i in (2, 8, 16, 24, 31):
        g3[i : i + 8, :] = columns_strided(rows_blurred(g2, 0, 2 * i, 8), 1) * (1.0 / 256.0)


def anchor_tile(base):
    return (iota((HALF, LANES), 0) + base).astype(F32)


def phase_table():
    source = iota((256, 256), 0)
    target = iota((256, 256), 1)
    return jnp.where(source == 4 * (target % 64) + target // 64, 1.0, 0.0).astype(jnp.bfloat16)


def phases_of(block, table):
    count = block.shape[0]
    split = select_columns(jnp.concatenate([block[:, :256], block[:, 256:]], axis=0), table)
    low_half = iota((count, LANES), 1) < 64
    found = []
    for pair in range(2):
        a = split[:count, pair * LANES : (pair + 1) * LANES]
        b = split[count:, pair * LANES : (pair + 1) * LANES]
        found += [jnp.where(low_half, a, right(b, 64)), jnp.where(low_half, right(a, 64), b)]
    return found


def hat(place, channel):
    return jnp.maximum(0.0, 1.0 - jnp.abs(place - channel))


def eight_totals(parts):
    sublane = iota((HALF, LANES), 0)

    def join(a, b, offset, span):
        mine = (sublane - offset + HALF) % (2 * span) < span
        return jnp.where(mine, a, b) + pltpu.roll(jnp.where(mine, b, a), HALF - span, axis=0)

    def four(a, b, c, d, offset):
        return join(join(a, b, offset, 4), join(c, d, offset + 2, 4), offset, 2)

    x = parts
    return join(four(x[0], x[4], x[2], x[6], 0), four(x[1], x[5], x[3], x[7], 1), 0, 1)


def rows_up(before, here, after):
    later = here + after
    return here + 0.25 * ((before + here) + later), later


def raised(rows):
    sums = [a + b for a, b in zip(rows, rows[1:])]
    out = []
    for n in range(1, len(rows) - 1):
        out += [rows[n] + 0.25 * (sums[n - 1] + sums[n]), sums[n]]
    return out


def two_phases(m, y, p):
    return y + 0.25 * ((m + y) + (y + p)), y + p


def four_phases(m, q0, q1, p):
    t0, t1, tm = q0 + q1, q1 + p, m + q0
    return q0 + 0.25 * (tm + t0), t0, q1 + 0.25 * (t0 + t1), t1


def sums_of_level_zero(d1, x15, sums):
    channel = [anchor_tile(HALF * g) for g in range(2)]

    def level_zero(t, carry):
        parts = [[None] * 8 for c in range(4)]
        for g in range(2):
            rows = [[d1[4 * t + 47 + n, 2 * g + c] for n in range(6)] for c in range(2)]
            fine = [raised(y) for y in ([right(y) for y in rows[1]], rows[0], rows[1], [left(y) for y in rows[0]])]
            for n in range(8):
                ups = four_phases(*[f[n] for f in fine])
                for c in range(4):
                    part = hat(spread(x15, c, 8 * t + n), channel[g]) * ups[c]
                    parts[c][n] = part if g == 0 else parts[c][n] + part
        for c in range(4):
            sums[c, pl.ds(8 * t, 8), :] = eight_totals(parts[c])
        return carry

    return level_zero


def sums_in_a(d1, d2, x15, g1, sums, c1a):
    channel = [anchor_tile(HALF * g) for g in range(2)]

    def level_one(t, carry):
        parts = [[None] * 8 for c in range(2)]
        for g in range(2):
            rows = [d2[4 * t + 22 + n, g] for n in range(6)]
            fine = [raised(y) for y in ([right(y) for y in rows], rows, [left(y) for y in rows])]
            for n in range(8):
                ups = two_phases(*[f[n] for f in fine])
                for c in range(2):
                    x = 8 * t + 46 + n
                    part = hat(spread(g1, c, x) * 15.0, channel[g]) * (d1[x, 2 * g + c] * 1024.0 - ups[c])
                    parts[c][n] = part if g == 0 else parts[c][n] + part
        for c in range(2):
            c1a[c, pl.ds(8 * t + 46, 8), :] = eight_totals(parts[c])
        return carry

    loop(0, 9, UNROLL_SUMS, level_one)

    level_zero = sums_of_level_zero(d1, x15, sums)
    level_zero(0, ())
    level_zero(15, ())


def kernel_z(block, x15, base_term, near_left, near_right, piece_left, piece_right, d1, sums, lum, mid, arrived):
    copies = []
    for q in range(4):
        rows = pl.ds(32 * q, 32)
        copies.append(pltpu.make_async_copy(block.at[rows, :], mid.at[rows, :], arrived.at[q]))
        copies[-1].start()
    table = phase_table()
    for copy in copies:
        copy.wait()
    for c, part in enumerate(phases_of(mid[...], table)):
        x15[c] = part * 15.0
        lum[c] = part * BETA
    near_left[...] = mid[:, :LANES]
    near_right[...] = mid[:, 384:]
    for n in range(3):
        rows = slice(80 * n, 80 * n + 80)
        piece_left[rows, :] = right(mid[48:, :LANES], 96 - 32 * n)
        piece_right[rows, :] = right(mid[48:, 384:], 96 - 32 * n)

    def natural(t, carry):
        rows = pl.ds(pl.multiple_of(8 * t, 8), 8)
        value = mid[rows, :]
        place = value * 15.0
        lower = jnp.floor(place)
        part = place - lower
        near = value - lower * STEP
        far = value - (lower + 1.0) * STEP
        bend = (1.0 - part) * near * jnp.exp(near * near * -800.0) + part * far * jnp.exp(far * far * -800.0)
        base_term[rows, :] = 0.5 * value + bend
        return carry

    loop(0, 16, 8, natural)
    anchors = [anchor_tile(HALF * g) * (BETA * STEP) for g in range(2)]
    first_level(lum, anchors, d1, 49, 111, 31, above=96)
    loop(1, 15, 7, sums_of_level_zero(d1, x15, sums))


def outer_phases(top, bottom, lum):
    table = phase_table()
    outer = jnp.concatenate([top[32:, :], bottom[:96, :]], axis=0)
    for c, part in enumerate(phases_of(outer, table)):
        lum[c, :96, :] = part[:96] * BETA
        lum[c, 224:, :] = part[96:] * BETA


def upper_rows(lum, d1):
    first_level(lum, [anchor_tile(HALF * g) * (BETA * STEP) for g in range(2)], d1, 2, 2 + EARLY, EARLY)


def kernel_p(early, top, bottom, middle, piece, d1_in, send_left, lum, d1):
    lane = iota((240, LANES), 1)
    direct = jnp.concatenate([top[32:, :LANES], middle[:48, :], bottom[:96, :LANES]], axis=0)
    send_left[...] = jnp.where(lane < 96, direct, piece[...])

    @pl.when(early[0] == 1)
    def _():
        outer_phases(top, bottom, lum)
        upper_rows(lum, d1)


def kernel_a(early, top, bottom, x15, lum_in, d1_in, sums_in, lum, d1, d2, d3, g1, g2, g3, sums, c1a):
    @pl.when(early[0] == 0)
    def _():
        outer_phases(top, bottom, lum)
        upper_rows(lum, d1)

    for c in range(4):
        lum[c, 96:224, :] = x15[c] * (BETA * STEP)
    guide_chain(lum, 1.0 / BETA, g1, g2, g3)
    anchors = [anchor_tile(HALF * g) * (BETA * STEP) for g in range(2)]
    first_level(lum, anchors, d1, 2 + EARLY, 49, 47 - EARLY)
    first_level(lum, anchors, d1, 111, 159, 24)
    next_levels(d1, d2, d3, 2)
    sums_in_a(d1, d2, x15, g1, sums, c1a)


def kernel_b(
    gain_ref, far_left, near_left, near_right, far_right,
    d2, d3, g1, g2, g3, base_term, sums, c1a, out,
    lum, s1, s2, s3, h1, h2, h3, b3, b4, b5, e3, e4, e5,
    c4, c3, c2a, c2s, c1s, sums_s, r5, r4, u4, r3, u3, wide3, w2, r2a, r2s, wide_a, wide_s, rest,
):
    gains = [gain_ref[i] for i in range(5)]
    lane = iota((HALF, LANES), 1)
    channel = [anchor_tile(HALF * g) for g in range(2)]
    split = anchor_tile(0) + jnp.where(lane >= 64, 8.0, 0.0)

    source = iota((512, 256), 0)
    target = iota((512, 256), 1)
    wanted = 32 + 320 * ((target // 32) % 2) + 4 * (target % 32) + target // 64
    table = jnp.where(source == wanted, 1.0, 0.0).astype(jnp.bfloat16)
    def unpacked(ref, low, high):
        a, b, c = [right(ref[80 * n : 80 * n + 80, :], 32 + 32 * n) for n in range(3)]
        at_lane = iota((80, LANES), 1)
        inner = jnp.where(at_lane < low, a, jnp.where(at_lane < high, b, c))
        return jnp.concatenate([ref[:144, :], inner, ref[144:, :]], axis=0)

    whole_left, whole_right = unpacked(far_left, 64, 96), unpacked(far_right, 32, 64)
    count = 160
    for start in range(0, ROWS, count):
        part = slice(start, start + count)
        natural = [whole_left[part], near_left[part, :], near_right[part, :], whole_right[part]]
        pieces = select_columns(jnp.concatenate(natural, axis=1), table)
        low_half = iota((count, LANES), 1) < 64
        for pair in range(2):
            a = pieces[:, pair * LANES : (pair + 1) * LANES] * BETA
            b = right(a, 64)
            lum[2 * pair, start : start + count, :] = jnp.where(low_half, a, b)
            lum[2 * pair + 1, start : start + count, :] = jnp.where(low_half, b, a)
    guide_chain(lum, 1.0 / BETA, h1, h2, h3)
    first_level(lum, [split * (BETA * STEP)], s1, 2, 159, 53)
    next_levels(s1, s2, s3, 1)

    first, last = lane == 0, lane == 127
    turn = lambda x, source, to: pltpu.roll(x, (to - source) % LANES, axis=1)

    def ends(x, t, low, high):
        return jnp.where(lane >= high, turn(t, 39, 127), jnp.where(lane <= low, turn(t, 24, 0), x))

    def edges_one(q0, q1, t0, t1):
        q0, q1 = ends(q0, t0, 2, 126), ends(q1, t1, 2, 126)
        return jnp.where(first, turn(t1, 23, 0), right(q1)), q0, q1, jnp.where(last, turn(t0, 40, 127), left(q0))

    def edges_two(y, t):
        y = ends(y, t, 1, 127)
        return jnp.where(first, turn(t, 23, 0), right(y)), y, jnp.where(last, turn(t, 40, 127), left(y))

    from_a = (lane >= 14) & (lane <= 74)
    index_a = jnp.clip(2 * (lane - 12), 0, 127)
    index_s = [jnp.clip(64 * g + jnp.where(lane < 14, 2 * lane, 2 * lane - 112), 0, 127) for g in range(2)]

    def merge(i, carry):
        for g in range(2):
            b3[i, g] = jnp.where(from_a, pick(d3[i, g], index_a), pick(s3[i, 0], index_s[g])) * (
                1.0 / (BETA * 2.0**24)
            )
        return carry

    loop(2, 39, 8, merge)
    for t in range(5):
        rows = slice(8 * t, 8 * t + 8)
        e3[rows, :] = jnp.where(from_a, pick(g3[rows, :], index_a), pick(h3[rows, :], index_s[0]))

    def fourth_level(i, carry):
        for g in range(2):
            b4[i, g] = columns_strided(fold(*[b3[2 * i + s - 2, g] for s in range(5)]), 1) * (1.0 / 256.0)
        return carry

    loop(2, 19, 17, fourth_level)

    def fifth_level(i, carry):
        for g in range(2):
            b5[i, g] = columns_strided(fold(*[b4[2 * i + s - 2, g] for s in range(5)]), 2) * (1.0 / 256.0)
        return carry

    loop(2, 9, 7, fifth_level)
    blur = lambda ref, i: fold(*[ref[pl.ds(2 * i + s - 2, 8, stride=2), :] for s in range(5)])
    for i in (2, 8, 11):
        e4[i : i + 8, :] = columns_strided(blur(e3, i), 1) * (1.0 / 256.0)
    e5[2:10, :] = columns_strided(blur(e4, 2), 2) * (1.0 / 256.0)

    def lanes_up(y, n):
        even = 0.125 * (right(y, n) + left(y, n)) + 0.75 * y
        odd = 0.5 * (right(y, n // 2) + left(y, n // 2))
        return even, odd

    def on_grid(y, n, parity):
        even, odd = lanes_up(y, n)
        return jnp.where(parity, odd, even)

    parity_four = (lane % 4) != 0
    parity_three = (lane % 2) != 0

    def coefficient_b(fine, coarse, guide, sums, start, n, parity):
        parts = []
        for i in range(start // 2, start // 2 + 4):
            made = [rows_up(coarse[i - 1, g], coarse[i, g], coarse[i + 1, g]) for g in range(2)]
            for odd in range(2):
                x = 2 * i + odd
                place = spread(guide, x) * 15.0
                terms = [
                    hat(place, channel[g]) * (fine[x, g] - 0.5 * on_grid(made[g][odd], n, parity)) for g in range(2)
                ]
                parts.append(terms[0] + terms[1])
        sums[start : start + 8, :] = eight_totals(parts)

    for start in (4, 12):
        coefficient_b(b4, b5, e4, c4, start, 4, parity_four)
    for start in (10, 18, 26):
        coefficient_b(b3, b4, e3, c3, start, 2, parity_three)

    def raise_rows(src, dst, start, count, index=()):
        above = src[index + (pl.ds(start - 1, count), slice(None))]
        here = src[index + (pl.ds(start, count), slice(None))]
        below = src[index + (pl.ds(start + 1, count), slice(None))]
        even, odd = rows_up(above, here, below)
        dst[index + (pl.ds(2 * start, count, stride=2), slice(None))] = 0.5 * even
        dst[index + (pl.ds(2 * start + 1, count, stride=2), slice(None))] = 0.5 * odd

    r5[...] = e5[...] * (1.0 - 0.5 * gains[4])
    raise_rows(r5, u4, 1, 8)
    for t in range(3):
        rows = slice(8 * t, 8 * t + 8)
        value = gains[4] * (0.5 * e4[rows, :] + c4[rows, :]) + on_grid(u4[rows, :], 4, parity_four)
        r4[rows, :] = value - (0.5 * gains[3]) * e4[rows, :]
    raise_rows(r4, u3, 4, 8)
    raise_rows(r4, u3, 8, 8)
    for t in range(1, 4):
        rows = slice(8 * t, 8 * t + 8)
        value = gains[3] * (0.5 * e3[rows, :] + c3[rows, :]) + on_grid(u3[rows, :], 2, parity_three)
        r3[rows, :] = value - (0.5 * gains[2]) * e3[rows, :]

    base_a = lane // 2 + 12
    column_s = jnp.where((lane // 32) % 2 == 0, lane % 32 - 24 + 256, lane % 32 + 120 + 256)
    base_s = column_s // 2 - 128 + 12
    odd_column = (lane % 2) != 0
    clip = lambda x: jnp.clip(x, 0, 127)
    base_a, base_s = clip(base_a), clip(base_s)

    def expand(y, at):
        even, odd = 0.125 * (right(y) + left(y)) + 0.75 * y, 0.5 * (y + left(y))
        return jnp.where(odd_column, pick(odd, at), pick(even, at))

    scale_two = 2.0 / (BETA * 2.0**16)

    def widen(i, carry):
        for g in range(2):
            wide3[i, g] = expand(b3[i, g], base_a)
        wide3[i, 2] = on_grid(s3[i, 0], 2, odd_column) * (1.0 / (BETA * 2.0**24))
        return carry

    loop(10, 32, 11, widen)

    def coefficient_two(t, carry):
        fine = [raised([wide3[4 * t + 10 + n, g] for n in range(6)]) for g in range(3)]
        parts, side = [], []
        for n in range(8):
            x = 8 * t + 22 + n
            place = spread(g2, 0, x) * 15.0
            terms = [hat(place, channel[g]) * (d2[x, g] * scale_two - fine[g][n]) for g in range(2)]
            parts.append(terms[0] + terms[1])
            place = spread(h2, 0, x) * 15.0
            side.append(hat(place, split) * (s2[x, 0] * scale_two - fine[2][n]))
        rows = pl.ds(8 * t + 22, 8)
        c2a[rows, :] = 0.5 * eight_totals(parts)
        both = eight_totals(side)
        c2s[rows, :] = 0.5 * (both + right(both, 64))
        return carry

    loop(0, 5, UNROLL_SUMS, coefficient_two)
    for start in (8, 16, 24):
        raise_rows(r3, w2, start, 8)
    for t in range(2, 8):
        rows = slice(8 * t, 8 * t + 8)
        coarse = w2[rows, :]
        value = gains[2] * (0.5 * g2[0, rows, :] + c2a[rows, :]) + expand(coarse, base_a)
        r2a[rows, :] = value - (0.5 * gains[1]) * g2[0, rows, :]
        guide = h2[0, rows, :]
        value = gains[2] * (0.5 * guide + c2s[rows, :]) + expand(coarse, base_s)
        r2s[rows, :] = value - (0.5 * gains[1]) * guide

    def side_one(t, carry):
        rows = [s2[4 * t + 22 + n, 0] for n in range(6)]
        fine = [raised(y) for y in ([right(y) for y in rows], rows, [left(y) for y in rows])]
        parts = [[], []]
        for n in range(8):
            ups = two_phases(*[f[n] for f in fine])
            for c in range(2):
                x = 8 * t + 46 + n
                parts[c].append(hat(spread(h1, c, x) * 15.0, split) * (s1[x, c] * 1024.0 - ups[c]))
        for c in range(2):
            both = eight_totals(parts[c])
            c1s[c, pl.ds(8 * t + 46, 8), :] = both + right(both, 64)
        return carry

    loop(0, 9, UNROLL_SUMS, side_one)

    def side_zero(t, carry):
        rows = [[s1[4 * t + 47 + n, c] for n in range(6)] for c in range(2)]
        fine = [raised(y) for y in ([right(y) for y in rows[1]], rows[0], rows[1], [left(y) for y in rows[0]])]
        parts = [[] for c in range(4)]
        for n in range(8):
            ups = four_phases(*[f[n] for f in fine])
            for c in range(4):
                place = spread(lum, c, 8 * t + 96 + n) * (15.0 / BETA)
                parts[c].append(hat(place, split) * ups[c])
        for c in range(4):
            both = eight_totals(parts[c])
            both = both + right(both, 64)
            sums_s[c, pl.ds(pl.multiple_of(8 * t, 8), 8), :] = both
        return carry

    loop(0, 16, UNROLL_SUMS, side_zero)
    scale_one = gains[1] * (1.0 / (BETA * 2.0**18))
    for start in (20, 28, 36, 44, 52):
        raise_rows(r2a, wide_a, start, 8)
        raise_rows(r2s, wide_s, start, 8)

    def collapse_one(t, carry):
        rows = pl.ds(pl.multiple_of(8 * t, 8), 8)
        y, z = wide_a[rows, :], wide_s[rows, :]
        m, y, p = edges_two(y, z)
        ups_a = two_phases(m, y, p)
        ups_s = two_phases(right(z), z, left(z))
        found = []
        for c in range(2):
            guide = g1[c, rows, :]
            found.append(
                (0.5 * (gains[1] - gains[0])) * guide + scale_one * c1a[c, rows, :] + 0.5 * ups_a[c]
            )
        side = []
        for c in range(2):
            guide = h1[c, rows, :]
            side.append((0.5 * (gains[1] - gains[0])) * guide + scale_one * c1s[c, rows, :] + 0.5 * ups_s[c])
        found = edges_one(found[0], found[1], side[0], side[1])
        for n in range(4):
            rest_in[n, rows, :] = found[n]
        return carry

    rest_in = lum
    loop(5, 15, 10, collapse_one)

    scale_zero = gains[0] * (1.0 / (BETA * 2.0**10))
    source = iota((256, 256), 0)
    target = iota((256, 256), 1)
    inverse = jnp.where(target == 4 * (source % 64) + source // 64, 1.0, 0.0).astype(jnp.bfloat16)

    def collapse_zero(t, carry):
        start = pl.multiple_of(8 * t, 8)
        fine = []
        for n in range(4):
            rows = [rest_in[n, pl.ds(start + 47 + k, 8), :] for k in range(3)]
            fine.append(rows_up(*rows))
        for odd in range(2):
            ups = four_phases(*[f[odd] for f in fine])
            for c in range(4):
                rest[c, pl.ds(2 * start + odd, 8, stride=2), :] = 0.25 * ups[c]
        for c in range(4):
            for k in range(2):
                rows = pl.ds(pl.multiple_of(2 * start, 16) + 8 * k, 8)
                total = ends(sums[c, rows, :], sums_s[c, rows, :], 0, 127)
                rest[c, rows, :] = rest[c, rows, :] - scale_zero * total
        return carry

    loop(0, 8, 8, collapse_zero)
    low_half = iota((128, LANES), 1) < 64
    halves = [[], []]
    for pair in range(2):
        a, b = rest[2 * pair], rest[2 * pair + 1]
        halves[0].append(jnp.where(low_half, a, right(b, 64)))
        halves[1].append(jnp.where(low_half, right(a, 64), b))
    both = jnp.concatenate([jnp.concatenate(h, axis=1) for h in halves], axis=0)
    natural = select_columns(both, inverse)
    out[:, :256] = natural[:128] + gains[0] * base_term[:, :256]
    out[:, 256:] = natural[128:] + gains[0] * base_term[:, 256:]


def shape(*dims):
    return jax.ShapeDtypeStruct(dims, F32)


def vmem(*dims):
    return pltpu.VMEM(dims, F32)


def run_z(mid):
    whole = pl.BlockSpec(memory_space=pltpu.VMEM)
    return pl.pallas_call(
        kernel_z,
        out_shape=(
            shape(4, 128, LANES),
            shape(128, 512),
            shape(128, LANES),
            shape(128, LANES),
            shape(240, LANES),
            shape(240, LANES),
            shape(160, 4, HALF, LANES),
            shape(4, 128, LANES),
        ),
        in_specs=[pl.BlockSpec(memory_space=pltpu.HBM)],
        out_specs=(whole,) * 8,
        scratch_shapes=[vmem(4, 128, LANES), vmem(128, 512), pltpu.SemaphoreType.DMA((4,))],
        compiler_params=pltpu.CompilerParams(vmem_limit_bytes=40 << 20),
        cost_estimate=pl.CostEstimate(flops=30_000_000, transcendentals=1_100_000, bytes_accessed=2_000_000),
    )(mid)


def run_p(early, top, bottom, middle, piece, d1):
    whole = pl.BlockSpec(memory_space=pltpu.VMEM)
    return pl.pallas_call(
        kernel_p,
        out_shape=(shape(240, LANES), shape(4, ROWS, LANES), shape(160, 4, HALF, LANES)),
        in_specs=[pl.BlockSpec(memory_space=pltpu.SMEM)] + [whole] * 5,
        out_specs=(whole,) * 3,
        input_output_aliases={5: 2},
        compiler_params=pltpu.CompilerParams(vmem_limit_bytes=40 << 20),
        cost_estimate=pl.CostEstimate(flops=30_000_000, transcendentals=1_000_000, bytes_accessed=3_000_000),
    )(early, top, bottom, middle, piece, d1)


def run_a(early, top, bottom, x15, lum, d1, sums):
    whole = pl.BlockSpec(memory_space=pltpu.VMEM)
    return pl.pallas_call(
        kernel_a,
        out_shape=(
            shape(4, ROWS, LANES),
            shape(160, 4, HALF, LANES),
            shape(80, 2, HALF, LANES),
            shape(40, 2, HALF, LANES),
            shape(2, 160, LANES),
            shape(1, 80, LANES),
            shape(40, LANES),
            shape(4, 128, LANES),
            shape(2, 160, LANES),
        ),
        in_specs=[pl.BlockSpec(memory_space=pltpu.SMEM)] + [whole] * 6,
        out_specs=(whole,) * 9,
        input_output_aliases={4: 0, 5: 1, 6: 7},
        compiler_params=pltpu.CompilerParams(vmem_limit_bytes=40 << 20),
        cost_estimate=pl.CostEstimate(flops=1_000, transcendentals=0, bytes_accessed=1_000),
    )(early, top, bottom, x15, lum, d1, sums)


def run_b(gain, *arrays):
    whole = pl.BlockSpec(memory_space=pltpu.VMEM)
    return pl.pallas_call(
        kernel_b,
        out_shape=shape(128, 512),
        in_specs=[pl.BlockSpec(memory_space=pltpu.SMEM)] + [whole] * len(arrays),
        out_specs=whole,
        scratch_shapes=[
            vmem(4, ROWS, LANES),
            vmem(160, 2, HALF, LANES),
            vmem(80, 1, HALF, LANES),
            vmem(40, 1, HALF, LANES),
            vmem(2, 160, LANES),
            vmem(1, 80, LANES),
            vmem(40, LANES),
            vmem(40, 2, HALF, LANES),
            vmem(24, 2, HALF, LANES),
            vmem(16, 2, HALF, LANES),
            vmem(40, LANES),
            vmem(24, LANES),
            vmem(16, LANES),
            vmem(24, LANES),
            vmem(40, LANES),
            vmem(80, LANES),
            vmem(80, LANES),
            vmem(2, 160, LANES),
            vmem(4, 128, LANES),
            vmem(16, LANES),
            vmem(24, LANES),
            vmem(24, LANES),
            vmem(40, LANES),
            vmem(40, LANES),
            vmem(40, 3, HALF, LANES),
            vmem(80, LANES),
            vmem(80, LANES),
            vmem(80, LANES),
            vmem(160, LANES),
            vmem(160, LANES),
            vmem(4, 128, LANES),
        ],
        compiler_params=pltpu.CompilerParams(vmem_limit_bytes=48 << 20),
        cost_estimate=pl.CostEstimate(flops=60_000_000, transcendentals=1_300_000, bytes_accessed=6_000_000),
    )(gain, *arrays)


def ring(axis, shift):
    count = lax.axis_size(axis)
    return [(i, (i + shift) % count) for i in range(count)]


def local(luminance, level_gain):
    top = lax.ppermute(luminance, "row", ring("row", 1))
    bottom = lax.ppermute(luminance, "row", ring("row", -1))
    x15, base_term, mid_left, mid_right, piece_left, piece_right, d1, sums = run_z(pltpu.with_memory_space_constraint(luminance, pltpu.HBM))
    lane = lax.broadcasted_iota(jnp.int32, (240, LANES), 1)

    def strip(columns, middle):
        return [top[32:, columns], middle, bottom[:96, columns]]

    first, last = slice(0, LANES), slice(384, 512)
    near_left, near_right = [jnp.concatenate(strip(*x), axis=0) for x in ((first, mid_left), (last, mid_right))]
    send_right = jnp.where(lane >= 32, jnp.concatenate(strip(last, mid_right[:48]), axis=0), piece_right)
    far_left = lax.ppermute(send_right, "col", ring("col", 1))
    piece_left, send_right = lax.optimization_barrier((piece_left, send_right))
    early = (lax.axis_index("col") == 0).astype(jnp.int32)[None]
    send_left, lum, d1 = run_p(early, top, bottom, mid_left, piece_left, d1)
    far_right = lax.ppermute(send_left, "col", ring("col", -1))
    _, d1, d2, d3, g1, g2, g3, sums, c1a = run_a(early, top, bottom, x15, lum, d1, sums)
    return run_b(
        level_gain, far_left, near_left, near_right, far_right, d2, d3, g1, g2, g3, base_term, sums, c1a
    )


def solution(mesh):
    return jax.shard_map(
        local, mesh=mesh, in_specs=(P("row", "col"), P()), out_specs=P("row", "col"), check_vma=False
    )
```

```python
import math

import jax
import jax.numpy as jnp
from jax import lax
from jax.experimental import pallas as pl
from jax.experimental.pallas import tpu as pltpu
from jax.sharding import PartitionSpec as P


ROWS = 320
LANES = 128
HALF = 8
STEP = 1.0 / 15.0
BETA = math.sqrt(800.0 * math.log2(math.e))
F32 = jnp.float32
UNROLL_TWO = {1: 77, 2: 39}
UNROLL_SUMS = 8
EARLY = 28


def iota(shape, dim):
    return lax.broadcasted_iota(jnp.int32, shape, dim)


def left(x, n=1):
    return pltpu.roll(x, LANES - n, axis=x.ndim - 1)


def right(x, n=1):
    return pltpu.roll(x, n, axis=x.ndim - 1)


def pick(x, idx):
    return jnp.take_along_axis(x, idx, axis=1)


def select_columns(x, table):
    hi = x.astype(jnp.bfloat16)
    rest = x - hi.astype(F32)
    mid = rest.astype(jnp.bfloat16)
    low = (rest - mid.astype(F32)).astype(jnp.bfloat16)
    count = x.shape[0]
    out = jnp.dot(jnp.concatenate([hi, mid, low], axis=0), table, preferred_element_type=F32)
    return out[:count] + out[count : 2 * count] + out[2 * count :]


def spread(ref, *index):
    return ref[index[:-1] + (pl.ds(index[-1], HALF, stride=0), slice(None))]


def fold(y0, y1, y2, y3, y4):
    return (y0 + y4) + 6.0 * y2 + 4.0 * (y1 + y3)


def bump(lum, anchor, power):
    u = lum - anchor
    return u * jnp.exp2(power - u * u)


def columns_from_four(y):
    y0, y1, y2, y3 = y
    return (
        (right(y2) + y2) + 6.0 * y0 + (right(y3) + y1),
        (y0 + left(y0)) + 6.0 * y2 + (y1 + y3),
    )


def columns_from_two(y):
    y0, y1 = y
    return fold(right(y0), right(y1), y0, y1, left(y0))


def columns_strided(y, n):
    return fold(right(y, 2 * n), right(y, n), y, left(y, n), left(y, 2 * n))


def loop(low, high, size, body, state=()):
    whole = (high - low) // size

    def several(t, state):
        for n in range(size):
            state = body(low + size * t + n, state)
        return state

    state = lax.fori_loop(0, whole, several, state)
    for i in range(low + size * whole, high):
        state = body(i, state)
    return state


def first_level(lum, anchors, d1, low, high, size, above=0):
    groups = len(anchors)

    def row(e, odd):
        values = [spread(lum, c, e - above) for c in range(4)]
        return [[bump(v, a, 2.0 * odd + 2.0 * (c % 2)) for c, v in enumerate(values)] for a in anchors]

    def step(i, state):
        even_before, even, odd_before = state
        odd = row(2 * i + 1, 1)
        even_next = row(2 * i + 2, 0)
        for g in range(groups):
            y = [
                (even_before[g][c] + even_next[g][c]) + 6.0 * even[g][c] + (odd_before[g][c] + odd[g][c])
                for c in range(4)
            ]
            out = columns_from_four(y)
            d1[i, 2 * g] = out[0]
            d1[i, 2 * g + 1] = out[1]
        return even, even_next, odd

    loop(low, high, size, step, (row(2 * low - 2, 0), row(2 * low, 0), row(2 * low - 1, 1)))


def next_levels(d1, d2, d3, groups):
    def second_level(i, carry):
        for g in range(groups):
            y = [fold(*[d1[2 * i + s - 2, 2 * g + c] for s in range(5)]) for c in range(2)]
            d2[i, g] = columns_from_two(y)
        return carry

    loop(2, 79, UNROLL_TWO[groups], second_level)

    def third_level(i, carry):
        for g in range(groups):
            d3[i, g] = columns_strided(fold(*[d2[2 * i + s - 2, g] for s in range(5)]), 1)
        return carry

    loop(2, 39, UNROLL_TWO[groups], third_level)


def rows_blurred(ref, c, base, count):
    return fold(*[ref[c, pl.ds(base + s - 2, count, stride=2), :] for s in range(5)])


def guide_chain(lum, scale, g1, g2, g3):
    def first(t, carry):
        i = pl.multiple_of(8 * t, 8) + 8
        y = [rows_blurred(lum, c, 2 * i, 8) * (1.0 + 3.0 * (c % 2)) for c in range(4)]
        out = columns_from_four(y)
        g1[0, pl.ds(i, 8), :] = out[0] * (scale / 256.0)
        g1[1, pl.ds(i, 8), :] = out[1] * (scale / 256.0)
        return carry

    loop(0, 18, 6, first)
    for i in (1, 151):
        y = [rows_blurred(lum, c, 2 * i, 8) * (1.0 + 3.0 * (c % 2)) for c in range(4)]
        out = columns_from_four(y)
        g1[0, i : i + 8, :] = out[0] * (scale / 256.0)
        g1[1, i : i + 8, :] = out[1] * (scale / 256.0)
    for i in (2, 8, 16, 24, 32, 40, 48, 56, 64, 71):
        y = [rows_blurred(g1, c, 2 * i, 8) for c in range(2)]
        g2[0, i : i + 8, :] = columns_from_two(y) * (1.0 / 256.0)
    for i in (2, 8, 16, 24, 31):
        g3[i : i + 8, :] = columns_strided(rows_blurred(g2, 0, 2 * i, 8), 1) * (1.0 / 256.0)


def anchor_tile(base):
    return (iota((HALF, LANES), 0) + base).astype(F32)


def phase_table():
    source = iota((256, 256), 0)
    target = iota((256, 256), 1)
    return jnp.where(source == 4 * (target % 64) + target // 64, 1.0, 0.0).astype(jnp.bfloat16)


def phases_of(block, table):
    count = block.shape[0]
    split = select_columns(jnp.concatenate([block[:, :256], block[:, 256:]], axis=0), table)
    low_half = iota((count, LANES), 1) < 64
    found = []
    for pair in range(2):
        a = split[:count, pair * LANES : (pair + 1) * LANES]
        b = split[count:, pair * LANES : (pair + 1) * LANES]
        found += [jnp.where(low_half, a, right(b, 64)), jnp.where(low_half, right(a, 64), b)]
    return found


def hat(place, channel):
    return jnp.maximum(0.0, 1.0 - jnp.abs(place - channel))


def eight_totals(parts):
    sublane = iota((HALF, LANES), 0)

    def join(a, b, offset, span):
        mine = (sublane - offset + HALF) % (2 * span) < span
        return jnp.where(mine, a, b) + pltpu.roll(jnp.where(mine, b, a), HALF - span, axis=0)

    def four(a, b, c, d, offset):
        return join(join(a, b, offset, 4), join(c, d, offset + 2, 4), offset, 2)

    x = parts
    return join(four(x[0], x[4], x[2], x[6], 0), four(x[1], x[5], x[3], x[7], 1), 0, 1)


def rows_up(before, here, after):
    later = here + after
    return here + 0.25 * ((before + here) + later), later


def raised(rows):
    sums = [a + b for a, b in zip(rows, rows[1:])]
    out = []
    for n in range(1, len(rows) - 1):
        out += [rows[n] + 0.25 * (sums[n - 1] + sums[n]), sums[n]]
    return out


def two_phases(m, y, p):
    return y + 0.25 * ((m + y) + (y + p)), y + p


def four_phases(m, q0, q1, p):
    t0, t1, tm = q0 + q1, q1 + p, m + q0
    return q0 + 0.25 * (tm + t0), t0, q1 + 0.25 * (t0 + t1), t1


def sums_of_level_zero(d1, x15, sums):
    channel = [anchor_tile(HALF * g) for g in range(2)]

    def level_zero(t, carry):
        parts = [[None] * 8 for c in range(4)]
        for g in range(2):
            rows = [[d1[4 * t + 47 + n, 2 * g + c] for n in range(6)] for c in range(2)]
            fine = [raised(y) for y in ([right(y) for y in rows[1]], rows[0], rows[1], [left(y) for y in rows[0]])]
            for n in range(8):
                ups = four_phases(*[f[n] for f in fine])
                for c in range(4):
                    part = hat(spread(x15, c, 8 * t + n), channel[g]) * ups[c]
                    parts[c][n] = part if g == 0 else parts[c][n] + part
        for c in range(4):
            sums[c, pl.ds(8 * t, 8), :] = eight_totals(parts[c])
        return carry

    return level_zero


def sums_in_a(d1, d2, x15, g1, sums, c1a):
    channel = [anchor_tile(HALF * g) for g in range(2)]

    def level_one(t, carry):
        parts = [[None] * 8 for c in range(2)]
        for g in range(2):
            rows = [d2[4 * t + 22 + n, g] for n in range(6)]
            fine = [raised(y) for y in ([right(y) for y in rows], rows, [left(y) for y in rows])]
            for n in range(8):
                ups = two_phases(*[f[n] for f in fine])
                for c in range(2):
                    x = 8 * t + 46 + n
                    part = hat(spread(g1, c, x) * 15.0, channel[g]) * (d1[x, 2 * g + c] * 1024.0 - ups[c])
                    parts[c][n] = part if g == 0 else parts[c][n] + part
        for c in range(2):
            c1a[c, pl.ds(8 * t + 46, 8), :] = eight_totals(parts[c])
        return carry

    loop(0, 9, UNROLL_SUMS, level_one)

    level_zero = sums_of_level_zero(d1, x15, sums)
    level_zero(0, ())
    level_zero(15, ())


def kernel_z(block, x15, base_term, near_left, near_right, piece_left, piece_right, d1, sums, lum, mid, arrived):
    copies = []
    for q in range(4):
        rows = pl.ds(32 * q, 32)
        copies.append(pltpu.make_async_copy(block.at[rows, :], mid.at[rows, :], arrived.at[q]))
        copies[-1].start()
    table = phase_table()
    for copy in copies:
        copy.wait()
    for c, part in enumerate(phases_of(mid[...], table)):
        x15[c] = part * 15.0
        lum[c] = part * BETA
    near_left[...] = mid[:, :LANES]
    near_right[...] = mid[:, 384:]
    for n in range(3):
        rows = slice(80 * n, 80 * n + 80)
        piece_left[rows, :] = right(mid[48:, :LANES], 96 - 32 * n)
        piece_right[rows, :] = right(mid[48:, 384:], 96 - 32 * n)

    def natural(t, carry):
        rows = pl.ds(pl.multiple_of(8 * t, 8), 8)
        value = mid[rows, :]
        place = value * 15.0
        lower = jnp.floor(place)
        part = place - lower
        near = value - lower * STEP
        far = value - (lower + 1.0) * STEP
        bend = (1.0 - part) * near * jnp.exp(near * near * -800.0) + part * far * jnp.exp(far * far * -800.0)
        base_term[rows, :] = 0.5 * value + bend
        return carry

    loop(0, 16, 8, natural)
    anchors = [anchor_tile(HALF * g) * (BETA * STEP) for g in range(2)]
    first_level(lum, anchors, d1, 49, 111, 31, above=96)
    loop(1, 15, 7, sums_of_level_zero(d1, x15, sums))


def outer_phases(top, bottom, lum):
    table = phase_table()
    outer = jnp.concatenate([top[32:, :], bottom[:96, :]], axis=0)
    for c, part in enumerate(phases_of(outer, table)):
        lum[c, :96, :] = part[:96] * BETA
        lum[c, 224:, :] = part[96:] * BETA


def upper_rows(lum, d1):
    first_level(lum, [anchor_tile(HALF * g) * (BETA * STEP) for g in range(2)], d1, 2, 2 + EARLY, EARLY)


def kernel_p(early, top, bottom, middle, piece, d1_in, send_left, lum, d1):
    lane = iota((240, LANES), 1)
    direct = jnp.concatenate([top[32:, :LANES], middle[:48, :], bottom[:96, :LANES]], axis=0)
    send_left[...] = jnp.where(lane < 96, direct, piece[...])

    @pl.when(early[0] == 1)
    def _():
        outer_phases(top, bottom, lum)
        upper_rows(lum, d1)


def kernel_a(early, top, bottom, x15, lum_in, d1_in, sums_in, lum, d1, d2, d3, g1, g2, g3, sums, c1a):
    @pl.when(early[0] == 0)
    def _():
        outer_phases(top, bottom, lum)
        upper_rows(lum, d1)

    for c in range(4):
        lum[c, 96:224, :] = x15[c] * (BETA * STEP)
    guide_chain(lum, 1.0 / BETA, g1, g2, g3)
    anchors = [anchor_tile(HALF * g) * (BETA * STEP) for g in range(2)]
    first_level(lum, anchors, d1, 2 + EARLY, 49, 47 - EARLY)
    first_level(lum, anchors, d1, 111, 159, 24)
    next_levels(d1, d2, d3, 2)
    sums_in_a(d1, d2, x15, g1, sums, c1a)


def kernel_b(
    gain_ref, far_left, near_left, near_right, far_right,
    d2, d3, g1, g2, g3, base_term, sums, c1a, out,
    lum, s1, s2, s3, h1, h2, h3, b3, b4, b5, e3, e4, e5,
    c4, c3, c2a, c2s, c1s, sums_s, r5, r4, u4, r3, u3, wide3, w2, r2a, r2s, wide_a, wide_s, rest,
):
    gains = [gain_ref[i] for i in range(5)]
    lane = iota((HALF, LANES), 1)
    channel = [anchor_tile(HALF * g) for g in range(2)]
    split = anchor_tile(0) + jnp.where(lane >= 64, 8.0, 0.0)

    source = iota((512, 256), 0)
    target = iota((512, 256), 1)
    wanted = 32 + 320 * ((target // 32) % 2) + 4 * (target % 32) + target // 64
    table = jnp.where(source == wanted, 1.0, 0.0).astype(jnp.bfloat16)
    def unpacked(ref, low, high):
        a, b, c = [right(ref[80 * n : 80 * n + 80, :], 32 + 32 * n) for n in range(3)]
        at_lane = iota((80, LANES), 1)
        inner = jnp.where(at_lane < low, a, jnp.where(at_lane < high, b, c))
        return jnp.concatenate([ref[:144, :], inner, ref[144:, :]], axis=0)

    whole_left, whole_right = unpacked(far_left, 64, 96), unpacked(far_right, 32, 64)
    count = 160
    for start in range(0, ROWS, count):
        part = slice(start, start + count)
        natural = [whole_left[part], near_left[part, :], near_right[part, :], whole_right[part]]
        pieces = select_columns(jnp.concatenate(natural, axis=1), table)
        low_half = iota((count, LANES), 1) < 64
        for pair in range(2):
            a = pieces[:, pair * LANES : (pair + 1) * LANES] * BETA
            b = right(a, 64)
            lum[2 * pair, start : start + count, :] = jnp.where(low_half, a, b)
            lum[2 * pair + 1, start : start + count, :] = jnp.where(low_half, b, a)
    guide_chain(lum, 1.0 / BETA, h1, h2, h3)
    first_level(lum, [split * (BETA * STEP)], s1, 2, 159, 79)
    next_levels(s1, s2, s3, 1)

    first, last = lane == 0, lane == 127
    turn = lambda x, source, to: pltpu.roll(x, (to - source) % LANES, axis=1)

    def ends(x, t, low, high):
        return jnp.where(lane >= high, turn(t, 39, 127), jnp.where(lane <= low, turn(t, 24, 0), x))

    def edges_one(q0, q1, t0, t1):
        q0, q1 = ends(q0, t0, 2, 126), ends(q1, t1, 2, 126)
        return jnp.where(first, turn(t1, 23, 0), right(q1)), q0, q1, jnp.where(last, turn(t0, 40, 127), left(q0))

    def edges_two(y, t):
        y = ends(y, t, 1, 127)
        return jnp.where(first, turn(t, 23, 0), right(y)), y, jnp.where(last, turn(t, 40, 127), left(y))

    from_a = (lane >= 14) & (lane <= 74)
    index_a = jnp.clip(2 * (lane - 12), 0, 127)
    index_s = [jnp.clip(64 * g + jnp.where(lane < 14, 2 * lane, 2 * lane - 112), 0, 127) for g in range(2)]

    def merge(i, carry):
        for g in range(2):
            b3[i, g] = jnp.where(from_a, pick(d3[i, g], index_a), pick(s3[i, 0], index_s[g])) * (
                1.0 / (BETA * 2.0**24)
            )
        return carry

    loop(2, 39, 8, merge)
    for t in range(5):
        rows = slice(8 * t, 8 * t + 8)
        e3[rows, :] = jnp.where(from_a, pick(g3[rows, :], index_a), pick(h3[rows, :], index_s[0]))

    def fourth_level(i, carry):
        for g in range(2):
            b4[i, g] = columns_strided(fold(*[b3[2 * i + s - 2, g] for s in range(5)]), 1) * (1.0 / 256.0)
        return carry

    loop(2, 19, 17, fourth_level)

    def fifth_level(i, carry):
        for g in range(2):
            b5[i, g] = columns_strided(fold(*[b4[2 * i + s - 2, g] for s in range(5)]), 2) * (1.0 / 256.0)
        return carry

    loop(2, 9, 7, fifth_level)
    blur = lambda ref, i: fold(*[ref[pl.ds(2 * i + s - 2, 8, stride=2), :] for s in range(5)])
    for i in (2, 8, 11):
        e4[i : i + 8, :] = columns_strided(blur(e3, i), 1) * (1.0 / 256.0)
    e5[2:10, :] = columns_strided(blur(e4, 2), 2) * (1.0 / 256.0)

    def lanes_up(y, n):
        even = 0.125 * (right(y, n) + left(y, n)) + 0.75 * y
        odd = 0.5 * (right(y, n // 2) + left(y, n // 2))
        return even, odd

    def on_grid(y, n, parity):
        even, odd = lanes_up(y, n)
        return jnp.where(parity, odd, even)

    parity_four = (lane % 4) != 0
    parity_three = (lane % 2) != 0

    def coefficient_b(fine, coarse, guide, sums, start, n, parity):
        parts = []
        for i in range(start // 2, start // 2 + 4):
            made = [rows_up(coarse[i - 1, g], coarse[i, g], coarse[i + 1, g]) for g in range(2)]
            for odd in range(2):
                x = 2 * i + odd
                place = spread(guide, x) * 15.0
                terms = [
                    hat(place, channel[g]) * (fine[x, g] - 0.5 * on_grid(made[g][odd], n, parity)) for g in range(2)
                ]
                parts.append(terms[0] + terms[1])
        sums[start : start + 8, :] = eight_totals(parts)

    for start in (4, 12):
        coefficient_b(b4, b5, e4, c4, start, 4, parity_four)
    for start in (10, 18, 26):
        coefficient_b(b3, b4, e3, c3, start, 2, parity_three)

    def raise_rows(src, dst, start, count, index=()):
        above = src[index + (pl.ds(start - 1, count), slice(None))]
        here = src[index + (pl.ds(start, count), slice(None))]
        below = src[index + (pl.ds(start + 1, count), slice(None))]
        even, odd = rows_up(above, here, below)
        dst[index + (pl.ds(2 * start, count, stride=2), slice(None))] = 0.5 * even
        dst[index + (pl.ds(2 * start + 1, count, stride=2), slice(None))] = 0.5 * odd

    r5[...] = e5[...] * (1.0 - 0.5 * gains[4])
    raise_rows(r5, u4, 1, 8)
    for t in range(3):
        rows = slice(8 * t, 8 * t + 8)
        value = gains[4] * (0.5 * e4[rows, :] + c4[rows, :]) + on_grid(u4[rows, :], 4, parity_four)
        r4[rows, :] = value - (0.5 * gains[3]) * e4[rows, :]
    raise_rows(r4, u3, 4, 8)
    raise_rows(r4, u3, 8, 8)
    for t in range(1, 4):
        rows = slice(8 * t, 8 * t + 8)
        value = gains[3] * (0.5 * e3[rows, :] + c3[rows, :]) + on_grid(u3[rows, :], 2, parity_three)
        r3[rows, :] = value - (0.5 * gains[2]) * e3[rows, :]

    base_a = lane // 2 + 12
    column_s = jnp.where((lane // 32) % 2 == 0, lane % 32 - 24 + 256, lane % 32 + 120 + 256)
    base_s = column_s // 2 - 128 + 12
    odd_column = (lane % 2) != 0
    clip = lambda x: jnp.clip(x, 0, 127)
    base_a, base_s = clip(base_a), clip(base_s)

    def expand(y, at):
        even, odd = 0.125 * (right(y) + left(y)) + 0.75 * y, 0.5 * (y + left(y))
        return jnp.where(odd_column, pick(odd, at), pick(even, at))

    scale_two = 2.0 / (BETA * 2.0**16)

    def widen(i, carry):
        for g in range(2):
            wide3[i, g] = expand(b3[i, g], base_a)
        wide3[i, 2] = on_grid(s3[i, 0], 2, odd_column) * (1.0 / (BETA * 2.0**24))
        return carry

    loop(10, 32, 11, widen)

    def coefficient_two(t, carry):
        fine = [raised([wide3[4 * t + 10 + n, g] for n in range(6)]) for g in range(3)]
        parts, side = [], []
        for n in range(8):
            x = 8 * t + 22 + n
            place = spread(g2, 0, x) * 15.0
            terms = [hat(place, channel[g]) * (d2[x, g] * scale_two - fine[g][n]) for g in range(2)]
            parts.append(terms[0] + terms[1])
            place = spread(h2, 0, x) * 15.0
            side.append(hat(place, split) * (s2[x, 0] * scale_two - fine[2][n]))
        rows = pl.ds(8 * t + 22, 8)
        c2a[rows, :] = 0.5 * eight_totals(parts)
        both = eight_totals(side)
        c2s[rows, :] = 0.5 * (both + right(both, 64))
        return carry

    loop(0, 5, UNROLL_SUMS, coefficient_two)
    for start in (8, 16, 24):
        raise_rows(r3, w2, start, 8)
    for t in range(2, 8):
        rows = slice(8 * t, 8 * t + 8)
        coarse = w2[rows, :]
        value = gains[2] * (0.5 * g2[0, rows, :] + c2a[rows, :]) + expand(coarse, base_a)
        r2a[rows, :] = value - (0.5 * gains[1]) * g2[0, rows, :]
        guide = h2[0, rows, :]
        value = gains[2] * (0.5 * guide + c2s[rows, :]) + expand(coarse, base_s)
        r2s[rows, :] = value - (0.5 * gains[1]) * guide

    def side_one(t, carry):
        rows = [s2[4 * t + 22 + n, 0] for n in range(6)]
        fine = [raised(y) for y in ([right(y) for y in rows], rows, [left(y) for y in rows])]
        parts = [[], []]
        for n in range(8):
            ups = two_phases(*[f[n] for f in fine])
            for c in range(2):
                x = 8 * t + 46 + n
                parts[c].append(hat(spread(h1, c, x) * 15.0, split) * (s1[x, c] * 1024.0 - ups[c]))
        for c in range(2):
            both = eight_totals(parts[c])
            c1s[c, pl.ds(8 * t + 46, 8), :] = both + right(both, 64)
        return carry

    loop(0, 9, UNROLL_SUMS, side_one)

    def side_zero(t, carry):
        rows = [[s1[4 * t + 47 + n, c] for n in range(6)] for c in range(2)]
        fine = [raised(y) for y in ([right(y) for y in rows[1]], rows[0], rows[1], [left(y) for y in rows[0]])]
        parts = [[] for c in range(4)]
        for n in range(8):
            ups = four_phases(*[f[n] for f in fine])
            for c in range(4):
                place = spread(lum, c, 8 * t + 96 + n) * (15.0 / BETA)
                parts[c].append(hat(place, split) * ups[c])
        for c in range(4):
            both = eight_totals(parts[c])
            both = both + right(both, 64)
            sums_s[c, pl.ds(pl.multiple_of(8 * t, 8), 8), :] = both
        return carry

    loop(0, 16, UNROLL_SUMS, side_zero)
    scale_one = gains[1] * (1.0 / (BETA * 2.0**18))
    for start in (20, 28, 36, 44, 52):
        raise_rows(r2a, wide_a, start, 8)
        raise_rows(r2s, wide_s, start, 8)

    def collapse_one(t, carry):
        rows = pl.ds(pl.multiple_of(8 * t, 8), 8)
        y, z = wide_a[rows, :], wide_s[rows, :]
        m, y, p = edges_two(y, z)
        ups_a = two_phases(m, y, p)
        ups_s = two_phases(right(z), z, left(z))
        found = []
        for c in range(2):
            guide = g1[c, rows, :]
            found.append(
                (0.5 * (gains[1] - gains[0])) * guide + scale_one * c1a[c, rows, :] + 0.5 * ups_a[c]
            )
        side = []
        for c in range(2):
            guide = h1[c, rows, :]
            side.append((0.5 * (gains[1] - gains[0])) * guide + scale_one * c1s[c, rows, :] + 0.5 * ups_s[c])
        found = edges_one(found[0], found[1], side[0], side[1])
        for n in range(4):
            rest_in[n, rows, :] = found[n]
        return carry

    rest_in = lum
    loop(5, 15, 10, collapse_one)

    scale_zero = gains[0] * (1.0 / (BETA * 2.0**10))
    source = iota((256, 256), 0)
    target = iota((256, 256), 1)
    inverse = jnp.where(target == 4 * (source % 64) + source // 64, 1.0, 0.0).astype(jnp.bfloat16)

    def collapse_zero(t, carry):
        start = pl.multiple_of(8 * t, 8)
        fine = []
        for n in range(4):
            rows = [rest_in[n, pl.ds(start + 47 + k, 8), :] for k in range(3)]
            fine.append(rows_up(*rows))
        for odd in range(2):
            ups = four_phases(*[f[odd] for f in fine])
            for c in range(4):
                rest[c, pl.ds(2 * start + odd, 8, stride=2), :] = 0.25 * ups[c]
        for c in range(4):
            for k in range(2):
                rows = pl.ds(pl.multiple_of(2 * start, 16) + 8 * k, 8)
                total = ends(sums[c, rows, :], sums_s[c, rows, :], 0, 127)
                rest[c, rows, :] = rest[c, rows, :] - scale_zero * total
        return carry

    loop(0, 8, 8, collapse_zero)
    low_half = iota((128, LANES), 1) < 64
    halves = [[], []]
    for pair in range(2):
        a, b = rest[2 * pair], rest[2 * pair + 1]
        halves[0].append(jnp.where(low_half, a, right(b, 64)))
        halves[1].append(jnp.where(low_half, right(a, 64), b))
    both = jnp.concatenate([jnp.concatenate(h, axis=1) for h in halves], axis=0)
    natural = select_columns(both, inverse)
    out[:, :256] = natural[:128] + gains[0] * base_term[:, :256]
    out[:, 256:] = natural[128:] + gains[0] * base_term[:, 256:]


def shape(*dims):
    return jax.ShapeDtypeStruct(dims, F32)


def vmem(*dims):
    return pltpu.VMEM(dims, F32)


def run_z(mid):
    whole = pl.BlockSpec(memory_space=pltpu.VMEM)
    return pl.pallas_call(
        kernel_z,
        out_shape=(
            shape(4, 128, LANES),
            shape(128, 512),
            shape(128, LANES),
            shape(128, LANES),
            shape(240, LANES),
            shape(240, LANES),
            shape(160, 4, HALF, LANES),
            shape(4, 128, LANES),
        ),
        in_specs=[pl.BlockSpec(memory_space=pltpu.HBM)],
        out_specs=(whole,) * 8,
        scratch_shapes=[vmem(4, 128, LANES), vmem(128, 512), pltpu.SemaphoreType.DMA((4,))],
        compiler_params=pltpu.CompilerParams(vmem_limit_bytes=40 << 20),
        cost_estimate=pl.CostEstimate(flops=30_000_000, transcendentals=1_100_000, bytes_accessed=2_000_000),
    )(mid)


def run_p(early, top, bottom, middle, piece, d1):
    whole = pl.BlockSpec(memory_space=pltpu.VMEM)
    return pl.pallas_call(
        kernel_p,
        out_shape=(shape(240, LANES), shape(4, ROWS, LANES), shape(160, 4, HALF, LANES)),
        in_specs=[pl.BlockSpec(memory_space=pltpu.SMEM)] + [whole] * 5,
        out_specs=(whole,) * 3,
        input_output_aliases={5: 2},
        compiler_params=pltpu.CompilerParams(vmem_limit_bytes=40 << 20),
        cost_estimate=pl.CostEstimate(flops=30_000_000, transcendentals=1_000_000, bytes_accessed=3_000_000),
    )(early, top, bottom, middle, piece, d1)


def run_a(early, top, bottom, x15, lum, d1, sums):
    whole = pl.BlockSpec(memory_space=pltpu.VMEM)
    return pl.pallas_call(
        kernel_a,
        out_shape=(
            shape(4, ROWS, LANES),
            shape(160, 4, HALF, LANES),
            shape(80, 2, HALF, LANES),
            shape(40, 2, HALF, LANES),
            shape(2, 160, LANES),
            shape(1, 80, LANES),
            shape(40, LANES),
            shape(4, 128, LANES),
            shape(2, 160, LANES),
        ),
        in_specs=[pl.BlockSpec(memory_space=pltpu.SMEM)] + [whole] * 6,
        out_specs=(whole,) * 9,
        input_output_aliases={4: 0, 5: 1, 6: 7},
        compiler_params=pltpu.CompilerParams(vmem_limit_bytes=40 << 20),
        cost_estimate=pl.CostEstimate(flops=1_000, transcendentals=0, bytes_accessed=1_000),
    )(early, top, bottom, x15, lum, d1, sums)


def run_b(gain, *arrays):
    whole = pl.BlockSpec(memory_space=pltpu.VMEM)
    return pl.pallas_call(
        kernel_b,
        out_shape=shape(128, 512),
        in_specs=[pl.BlockSpec(memory_space=pltpu.SMEM)] + [whole] * len(arrays),
        out_specs=whole,
        scratch_shapes=[
            vmem(4, ROWS, LANES),
            vmem(160, 2, HALF, LANES),
            vmem(80, 1, HALF, LANES),
            vmem(40, 1, HALF, LANES),
            vmem(2, 160, LANES),
            vmem(1, 80, LANES),
            vmem(40, LANES),
            vmem(40, 2, HALF, LANES),
            vmem(24, 2, HALF, LANES),
            vmem(16, 2, HALF, LANES),
            vmem(40, LANES),
            vmem(24, LANES),
            vmem(16, LANES),
            vmem(24, LANES),
            vmem(40, LANES),
            vmem(80, LANES),
            vmem(80, LANES),
            vmem(2, 160, LANES),
            vmem(4, 128, LANES),
            vmem(16, LANES),
            vmem(24, LANES),
            vmem(24, LANES),
            vmem(40, LANES),
            vmem(40, LANES),
            vmem(40, 3, HALF, LANES),
            vmem(80, LANES),
            vmem(80, LANES),
            vmem(80, LANES),
            vmem(160, LANES),
            vmem(160, LANES),
            vmem(4, 128, LANES),
        ],
        compiler_params=pltpu.CompilerParams(vmem_limit_bytes=48 << 20),
        cost_estimate=pl.CostEstimate(flops=60_000_000, transcendentals=1_300_000, bytes_accessed=6_000_000),
    )(gain, *arrays)


def ring(axis, shift):
    count = lax.axis_size(axis)
    return [(i, (i + shift) % count) for i in range(count)]


def local(luminance, level_gain):
    top = lax.ppermute(luminance, "row", ring("row", 1))
    bottom = lax.ppermute(luminance, "row", ring("row", -1))
    x15, base_term, mid_left, mid_right, piece_left, piece_right, d1, sums = run_z(pltpu.with_memory_space_constraint(luminance, pltpu.HBM))
    lane = lax.broadcasted_iota(jnp.int32, (240, LANES), 1)

    def strip(columns, middle):
        return [top[32:, columns], middle, bottom[:96, columns]]

    first, last = slice(0, LANES), slice(384, 512)
    near_left, near_right = [jnp.concatenate(strip(*x), axis=0) for x in ((first, mid_left), (last, mid_right))]
    send_right = jnp.where(lane >= 32, jnp.concatenate(strip(last, mid_right[:48]), axis=0), piece_right)
    far_left = lax.ppermute(send_right, "col", ring("col", 1))
    piece_left, send_right = lax.optimization_barrier((piece_left, send_right))
    early = (lax.axis_index("col") == 0).astype(jnp.int32)[None]
    send_left, lum, d1 = run_p(early, top, bottom, mid_left, piece_left, d1)
    far_right = lax.ppermute(send_left, "col", ring("col", -1))
    _, d1, d2, d3, g1, g2, g3, sums, c1a = run_a(early, top, bottom, x15, lum, d1, sums)
    return run_b(
        level_gain, far_left, near_left, near_right, far_right, d2, d3, g1, g2, g3, base_term, sums, c1a
    )


def solution(mesh):
    return jax.shard_map(
        local, mesh=mesh, in_specs=(P("row", "col"), P()), out_specs=P("row", "col"), check_vma=False
    )
```
